32 devices in a mesh: gx: 32 (over z, y, x, core).
Axes of the slice: x: 2, y: 2, z: 4, core: 2. Of those that a mesh axis runs over, the one named last changes fastest.
Arguments:
- hot_cache: bfloat16 [16384, 128], P('gx'), may hold values from -6 to 6
- cold_table: bfloat16 [262144, 128], P('gx'), may hold values from -6 to 6
- serve_index: int32 [32, 32, 32], P('gx'), may hold values from 0 to 8191
- serve_count: int32 [32, 32], P('gx'), may hold values from 1 to 32, as said below
- target_slot: int32 [4096, 11], P('gx'), may hold values from 0 to 17407, as said below
- hop2_slot: int32 [4096, 11, 15], P('gx'), may hold values from 0 to 17407, as said below
- hop1_count: int32 [4096], P('gx'), may hold values from 1 to 10
- hop2_count: int32 [4096, 11], P('gx'), may hold values from 1 to 15
- w_first: bfloat16 [256, 256], replicated, may hold values from -0.375 to 0.375
- b_first: float32 [256], replicated, may hold values from -3 to 3
- w_second: bfloat16 [512, 256], replicated, may hold values from -0.25 to 0.25
- b_second: float32 [256], replicated, may hold values from -3 to 3
Outputs:
- embedding: float32 [4096, 256], P('gx')
The draws below stay inside these ranges and needn't reach their ends.
Inputs may be any that keep to these rules, and one draw needn't show every extreme that they name: `serve_count`: live cold slots from owner o to device d; for every draw some owner sends 32 live rows to every device. A slot below 16384 is a hot-cache row, owned by device slot // 512; otherwise it is 16384 + o * 32 + j with j < serve_count[o, d], d the seed's device. Over all entries of target_slot and hop2_slot of one device's seeds, at most 64 distinct hot rows of any one owner appear, and some owner has exactly 64 for every device. `hop2_slot`: as target_slot.
All inputs are finite; a program needn't handle non-finite values.
Results may differ from the reference program's by a relative error of at most 0.0024.
Values may be sent and summed in bfloat16 or wider, within the bound.
No kernel may reach another device: no remote copies, remote signals or barrier semaphores. Data moves between devices by JAX's collectives and lax.ppermute only.
A program may use at most 128 MiB of HBM per device.

```python
import jax
import jax.numpy as jnp
from jax import lax

F = 128
H = 256
FAN1 = 10
FAN2 = 15
B_DEV = 128
HOT_DEV = 512
HOT_REQ = 64
COLD_DEV = 8192
REQ = 32
TARGETS = 11
SEEDS = 4096
HOT = 16384
COLD = 262144
N_GX = 32


def count_helper(key):
    count_key = jax.random.fold_in(key, 5)
    first_key, second_key, third_key = jax.random.split(count_key, 3)
    busy = jax.random.randint(first_key, (N_GX,), 0, 8) == 0
    limit = jnp.where(busy, REQ, max(REQ // 2, 1))
    counts = jax.random.randint(second_key, (N_GX, N_GX), 1, limit[:, None] + 1)
    chosen = jax.random.randint(third_key, (), 0, N_GX)
    counts = counts.at[chosen].set(REQ)
    return counts.astype(jnp.int32)


def slot_helper(key):
    counts = count_helper(key)
    slot_key = jax.random.fold_in(key, 11)
    key_one, key_two, key_three, key_four, key_five, key_six = jax.random.split(slot_key, 6)
    per_device = B_DEV * (FAN1 + 1) * (FAN2 + 1)
    shape_all = (N_GX, per_device)
    is_hot = jax.random.randint(key_one, shape_all, 0, 2)
    pick_hot = jax.random.randint(key_two, shape_all, 0, HOT_REQ)
    owner = jax.random.randint(key_three, shape_all, 0, N_GX)
    requester = jnp.arange(N_GX, dtype=jnp.int32)[:, None]
    position = jnp.arange(per_device, dtype=jnp.int32)[None, :]
    forced_owner = jax.random.randint(key_six, (N_GX,), 0, N_GX)
    forced = position < HOT_REQ
    is_hot = jnp.where(forced, 1, is_hot)
    owner = jnp.where(forced, forced_owner[:, None], owner)
    pick_hot = jnp.where(forced, position, pick_hot)
    offset = jax.random.randint(key_five, (N_GX, N_GX), 0, HOT_DEV)
    local_hot = (offset[requester, owner] + pick_hot) % HOT_DEV
    hot_pick = owner * HOT_DEV + local_hot
    limit = counts[owner, requester]
    cold_pick = jax.random.randint(key_four, shape_all, 0, limit)
    slots = jnp.where(is_hot == 1, hot_pick, HOT + owner * REQ + cold_pick).astype(jnp.int32)
    return slots.reshape(SEEDS, FAN1 + 1, FAN2 + 1)


def draw_serve_count(key, part):
    return count_helper(key)


def draw_target_slot(key, part):
    return slot_helper(key)[:, :, 0]


def draw_hop2_slot(key, part):
    return slot_helper(key)[:, :, 1:]


def plant(array, stream_key, low, largest):
    longest = array.shape.index(max(array.shape))
    spots = []
    for shift in (0, 1):
        where = [jax.random.randint(jax.random.fold_in(stream_key, axis), (), 0, length) for axis, length in enumerate(array.shape)]
        where[longest] = (where[longest] + shift) % array.shape[longest]
        spots.append(tuple(where))
    return array.at[spots[0]].set(low).at[spots[1]].set(largest)


def shard_levels(rng, shape, pieces, smallest, largest):
    loudness = 1.0
    for dim, blocks in pieces:
        draws = jax.random.uniform(jax.random.fold_in(jax.random.fold_in(rng, 6), dim), (blocks,), jnp.float32, smallest / len(pieces), largest / len(pieces))
        loudness = loudness * jnp.repeat(jnp.exp(draws), shape[dim] // blocks).reshape((-1,) + (1,) * (len(shape) - 1 - dim))
    return loudness


def scatter_about(stream_key, shape, scale, most, shards=(), kind=jnp.bfloat16):
    values = jax.random.normal(stream_key, shape, jnp.float32) * scale
    if len(shards) > 0:
        values = shard_levels(stream_key, shape, shards, -0.22, 0.18) * values
    return jnp.clip(values, min=-most, max=most).astype(kind)


def setup_inputs(seed: int = 0) -> dict:
    keys = jax.random.split(jax.random.key(seed), 13)
    hot_cache = scatter_about(keys[0], (HOT, F), 1.0, 6.0, ((0, 32),))
    cold_table = scatter_about(keys[1], (COLD, F), 1.0, 6.0, ((0, 32),))
    serve_index = plant(jax.random.randint(keys[2], (N_GX, N_GX, REQ), 0, COLD_DEV), jax.random.fold_in(keys[2], 1), 0, COLD_DEV - 1).astype(jnp.int32)
    serve_count = draw_serve_count(jax.random.fold_in(keys[12], 71), 0)
    target_slot = draw_target_slot(jax.random.fold_in(keys[12], 71), 0)
    hop2_slot = draw_hop2_slot(jax.random.fold_in(keys[12], 71), 0)
    hop1_count = plant(jax.random.randint(keys[6], (SEEDS,), 1, FAN1 + 1), jax.random.fold_in(keys[6], 1), 1, FAN1).astype(jnp.int32)
    hop2_count = plant(jax.random.randint(keys[7], (SEEDS, TARGETS), 1, FAN2 + 1), jax.random.fold_in(keys[7], 1), 1, FAN2).astype(jnp.int32)
    w_first = scatter_about(keys[8], (2 * F, H), (2 * F) ** -0.5, 0.375)
    b_first = scatter_about(keys[9], (H,), 0.5, 3.0, (), jnp.float32)
    w_second = scatter_about(keys[10], (2 * H, H), (2 * H) ** -0.5, 0.25)
    b_second = scatter_about(keys[11], (H,), 0.5, 3.0, (), jnp.float32)
    return dict(hot_cache=hot_cache, cold_table=cold_table, serve_index=serve_index, serve_count=serve_count, target_slot=target_slot, hop2_slot=hop2_slot, hop1_count=hop1_count, hop2_count=hop2_count, w_first=w_first, b_first=b_first, w_second=w_second, b_second=b_second)


def reduce_rows(picked, hop2_count):
    weights = (lax.broadcasted_iota(jnp.int32, hop2_count.shape + (picked.shape[2] - 1,), 2) < hop2_count[..., None]).astype(jnp.bfloat16)
    own_rows = picked[:, :, 0].astype(jnp.float32)
    neighbour_sum = jnp.einsum("btkf,btk->btf", picked[:, :, 1:], weights, preferred_element_type=jnp.float32)
    return own_rows, neighbour_sum


def layers(own_rows, neighbour_sum, hop1_count, hop2_count, w_first, b_first, w_second, b_second):
    aggregate = (neighbour_sum / hop2_count[..., None].astype(jnp.float32)).astype(jnp.bfloat16)
    stacked = jnp.concatenate([own_rows.astype(jnp.bfloat16), aggregate], -1)
    seed_rows, targets_here = stacked.shape[0], stacked.shape[1]
    hidden = jnp.dot(stacked.reshape(seed_rows * targets_here, -1), w_first, preferred_element_type=jnp.float32) + b_first
    hidden = jax.nn.relu(hidden).astype(jnp.bfloat16).reshape(seed_rows, targets_here, -1)
    first_mask = (lax.broadcasted_iota(jnp.int32, (seed_rows, targets_here - 1), 1) < hop1_count[:, None]).astype(jnp.bfloat16)
    pooled = jnp.einsum("bjh,bj->bh", hidden[:, 1:], first_mask, preferred_element_type=jnp.float32) / hop1_count[:, None].astype(jnp.float32)
    joined = jnp.concatenate([hidden[:, 0], pooled.astype(jnp.bfloat16)], -1)
    return jnp.dot(joined, w_second, preferred_element_type=jnp.float32) + b_second


def reference(hot_cache, cold_table, serve_index, serve_count, target_slot, hop2_slot, hop1_count, hop2_count, w_first, b_first, w_second, b_second):
    cold_blocks = cold_table.reshape(N_GX, COLD_DEV, F)
    owners = jnp.arange(N_GX, dtype=jnp.int32)[:, None]
    slot_iota = lax.broadcasted_iota(jnp.int32, (N_GX, REQ), 1)

    def one_device(device):
        wanted = serve_index[:, device, :]
        served = cold_blocks[owners, wanted]
        live = slot_iota < serve_count[:, device][:, None]
        served = jnp.where(live[..., None], served, jnp.zeros((), cold_table.dtype))
        table = jnp.concatenate([hot_cache, served.reshape(N_GX * REQ, F)], 0)
        first_row = (device * B_DEV).astype(jnp.int32)
        own_slot = lax.dynamic_slice_in_dim(target_slot, first_row, B_DEV, 0)
        near_slot = lax.dynamic_slice_in_dim(hop2_slot, first_row, B_DEV, 0)
        count_one = lax.dynamic_slice_in_dim(hop1_count, first_row, B_DEV, 0)
        count_two = lax.dynamic_slice_in_dim(hop2_count, first_row, B_DEV, 0)
        slots = jnp.concatenate([own_slot[..., None], near_slot], -1)
        own_rows, neighbour_sum = reduce_rows(table[slots], count_two)
        return layers(own_rows, neighbour_sum, count_one, count_two, w_first, b_first, w_second, b_second)

    outputs = lax.map(one_device, jnp.arange(N_GX, dtype=jnp.int32))
    return outputs.reshape(SEEDS, H)
```

```python
import functools

import jax
import jax.numpy as jnp
from jax import lax
from jax.experimental import pallas as pl
from jax.experimental.pallas import tpu as pltpu
from jax.sharding import PartitionSpec as P


def finish_kernel(
    slots, hop1, hot, cold, count_two, count_one, w_first, b_first, w_second, b_second,
    out, table, own, total, stage, sems,
):
    n_hot, n_cold = hot.shape[0], cold.shape[0]
    seeds, width = own.shape[1:]
    targets = count_two.shape[1]
    group = 2
    per = slots.shape[0] // (own.shape[0] * seeds)
    block = stage.shape[1]
    pieces = [(hot, i) for i in range(0, n_hot, block)]
    pieces += [(cold, i) for i in range(0, n_cold, block)]

    def fetch(p):
        ref, start = pieces[p]
        return pltpu.make_async_copy(
            ref.at[pl.ds(start, block)], stage.at[p % 2], sems.at[p % 2]
        )

    fetch(0).start()
    table[pl.ds(n_hot + n_cold, 8), :] = jnp.zeros((8, width), jnp.float32)
    for p in range(len(pieces)):
        if p + 1 < len(pieces):
            fetch(p + 1).start()
        fetch(p).wait()
        table[pl.ds(p * block, block), :] = stage[p % 2].astype(jnp.float32)

    def tree(rows):
        while len(rows) > 1:
            rows = [a + b for a, b in zip(rows[::2], rows[1::2])] + (
                [rows[-1]] if len(rows) % 2 else []
            )
        return rows[0]

    def one_seed(s, carry):
        def some_targets(i, inner):
            first = i * group
            base = first * (per * seeds) + s
            for g in range(group):
                near = [
                    table[pl.ds(slots[base + ((g * per + k) * seeds)], 1), :] for k in range(per)
                ]
                own[first + g, pl.ds(s, 1), :] = near[0]
                total[first + g, pl.ds(s, 1), :] = tree(near[1:])
            return inner

        return lax.fori_loop(0, (hop1[s] + group) // group, some_targets, carry)

    lax.fori_loop(0, seeds, one_seed, 0)

    pooled = jnp.zeros((seeds, w_first.shape[1]), jnp.float32)
    near = count_one[...]
    for t in range(targets):
        aggregate = (total[t] / count_two[:, t : t + 1].astype(jnp.float32)).astype(jnp.bfloat16)
        stacked = jnp.concatenate([own[t].astype(jnp.bfloat16), aggregate], -1)
        hidden = jnp.dot(stacked, w_first[...], preferred_element_type=jnp.float32) + b_first[...]
        hidden = jnp.maximum(hidden, 0.0).astype(jnp.bfloat16)
        if t == 0:
            seed_hidden = hidden
        else:
            pooled += jnp.where(near > t - 1, hidden.astype(jnp.float32), 0.0)
    pooled = (pooled / near.astype(jnp.float32)).astype(jnp.bfloat16)
    joined = jnp.concatenate([seed_hidden, pooled], -1)
    out[...] = jnp.dot(joined, w_second[...], preferred_element_type=jnp.float32) + b_second[...]


def finish(hot, cold, slots, hop1, hop2, w_first, b_first, w_second, b_second):
    seeds, targets = hop2.shape
    width = hot.shape[1]
    rows = hot.shape[0] + cold.shape[0]
    block = cold.shape[0]
    vmem = pl.BlockSpec(memory_space=pltpu.VMEM)
    smem = pl.BlockSpec(memory_space=pltpu.SMEM)
    anyspace = pl.BlockSpec(memory_space=pl.ANY)
    return pl.pallas_call(
        finish_kernel,
        out_shape=jax.ShapeDtypeStruct((seeds, w_second.shape[1]), jnp.float32),
        in_specs=[smem, smem, anyspace, anyspace] + [vmem] * 6,
        out_specs=vmem,
        scratch_shapes=[
            pltpu.VMEM((rows + 8, width), jnp.float32),
            pltpu.VMEM((targets + targets % 2, seeds, width), jnp.float32),
            pltpu.VMEM((targets + targets % 2, seeds, width), jnp.float32),
            pltpu.VMEM((2, block, width), hot.dtype),
            pltpu.SemaphoreType.DMA((2,)),
        ],
        name="finish",
    )(
        slots, hop1, hot, cold, hop2, hop1[:, None],
        w_first, b_first[None], w_second, b_second[None],
    )


def on_device(
    hot_cache, cold_table, serve_index, serve_count, target_slot, hop2_slot,
    hop1_count, hop2_count, w_first, b_first, w_second, b_second,
):
    served_index = serve_index[0]
    live_counts = serve_count[0]
    slot_iota = lax.broadcasted_iota(jnp.int32, served_index.shape, 1)
    served = cold_table[served_index]
    served = jnp.where(
        (slot_iota < live_counts[:, None])[..., None], served, jnp.zeros((), cold_table.dtype)
    )
    received = lax.all_to_all(served, "gx", split_axis=0, concat_axis=0, tiled=True)
    cold_block = received.reshape(-1, received.shape[2])
    hot_all = lax.all_gather(hot_cache, "gx", axis=0, tiled=True)
    empty_row = hot_all.shape[0] + cold_block.shape[0]
    near = jnp.transpose(hop2_slot, (1, 2, 0))
    live = lax.broadcasted_iota(jnp.int32, near.shape, 1) < hop2_count.T[:, None, :]
    slots = jnp.concatenate([target_slot.T[:, None, :], jnp.where(live, near, empty_row)], 1)
    slots = jnp.pad(slots, ((0, slots.shape[0] % 2), (0, 0), (0, 0))).reshape(-1)
    return finish(
        hot_all, cold_block, slots, hop1_count, hop2_count, w_first, b_first, w_second, b_second
    )


def solution(mesh):
    return jax.shard_map(
        on_device,
        mesh=mesh,
        in_specs=(
            P("gx", None), P("gx", None), P("gx", None, None), P("gx", None), P("gx", None),
            P("gx", None, None), P("gx"), P("gx", None), P(), P(), P(), P(),
        ),
        out_specs=P("gx", None),
        check_vma=False,
    )
```

```python
import functools

import jax
import jax.numpy as jnp
from jax import lax
from jax.experimental import pallas as pl
from jax.experimental.pallas import tpu as pltpu
from jax.sharding import PartitionSpec as P

LANES = 128
HOT_REQ = 64
TASKS = 4

VMEM = pl.BlockSpec(memory_space=pltpu.VMEM)
SMEM = pl.BlockSpec(memory_space=pltpu.SMEM)


def split(size):
    bits = size.bit_length() - 1
    assert size == 1 << bits
    return bits


def one_hot(index, size):
    iota = lax.broadcasted_iota(jnp.int32, (size, index.shape[1]), 0)
    return jnp.where(iota == index, 1.0, 0.0).astype(jnp.bfloat16)


def rank_kernel(own, near, rank):
    owners, lines = rank.shape[0], rank.shape[1]
    high = owners * lines
    bits = split(LANES)
    counts = jnp.zeros((high, LANES), jnp.float32)
    for t in range(own.shape[0]):
        rows = [own[t : t + 1, :]] + [near[t, k : k + 1, :] for k in range(near.shape[1])]
        outer = jnp.concatenate([one_hot(r >> bits, high) for r in rows], 1)
        inner = jnp.concatenate([one_hot(r & (LANES - 1), LANES) for r in rows], 1)
        counts += lax.dot_general(
            outer, inner, (((1,), (1,)), ((), ())), preferred_element_type=jnp.float32
        )
    used = counts > 0.0
    flags = jnp.where(used, 1.0, 0.0).astype(jnp.bfloat16)
    a = lax.broadcasted_iota(jnp.int32, (LANES, LANES), 0)
    b = lax.broadcasted_iota(jnp.int32, (LANES, LANES), 1)
    before = jnp.where(a < b, 1.0, 0.0).astype(jnp.bfloat16)
    inside = jnp.dot(flags, before, preferred_element_type=jnp.float32)
    every = jnp.ones((LANES, LANES), jnp.bfloat16)
    sums = jnp.dot(flags, every, preferred_element_type=jnp.float32).astype(jnp.bfloat16)
    a = lax.broadcasted_iota(jnp.int32, (high, high), 0)
    b = lax.broadcasted_iota(jnp.int32, (high, high), 1)
    line_bits = split(lines)
    earlier = (a > b) & ((a >> line_bits) == (b >> line_bits))
    earlier = jnp.where(earlier, 1.0, 0.0).astype(jnp.bfloat16)
    offset = jnp.dot(earlier, sums, preferred_element_type=jnp.float32)
    value = jnp.where(used, inside + offset, -1.0)
    rank[...] = value.reshape(rank.shape)


def select_kernel(group, asked, hot, cold, out):
    owners, lines = asked.shape[0], asked.shape[1]
    cold_rows = cold.shape[1]
    want = lax.broadcasted_iota(jnp.int32, (HOT_REQ, LANES), 0).astype(jnp.float32)

    def some(i, carry):
        picks = []
        for g in range(group):
            row = asked[i * group + g]
            picks.append(
                jnp.concatenate(
                    [jnp.where(want == row[r : r + 1, :], 1.0, 0.0) for r in range(lines)], 1
                ).astype(jnp.bfloat16)
            )
        picked = jnp.dot(
            jnp.concatenate(picks, 0), hot[...], preferred_element_type=jnp.float32
        ).astype(out.dtype)
        for g in range(group):
            d = i * group + g
            out[d, pl.ds(0, HOT_REQ), :] = picked[g * HOT_REQ : (g + 1) * HOT_REQ]
            out[d, pl.ds(HOT_REQ, cold_rows), :] = cold[d]
        return carry

    lax.fori_loop(0, owners // group, some, 0)


def remap_kernel(cold_rows, own, near, count, rank, out):
    owners, lines = rank.shape[0], rank.shape[1]
    high = owners * lines
    targets, fan = near.shape[0], near.shape[1]
    stride = out.shape[0] // (fan + 1)
    bits, line_bits, cold_bits = split(LANES), split(lines), split(cold_rows)
    per = HOT_REQ + cold_rows
    first_cold = high * LANES
    by_low = jnp.transpose(rank[...].reshape(high, LANES)).astype(jnp.bfloat16)
    low = lax.broadcasted_iota(jnp.int32, (LANES, LANES), 0)
    empty = jnp.full((1, LANES), owners * per, jnp.int32)
    for t in range(targets):
        rows = [own[t : t + 1, :]] + [near[t, k : k + 1, :] for k in range(fan)]
        outer = jnp.concatenate([one_hot(r >> bits, high) for r in rows], 1)
        found = jnp.dot(by_low, outer, preferred_element_type=jnp.float32)
        for k, r in enumerate(rows):
            mine = jnp.where(
                low == (r & (LANES - 1)), found[:, k * LANES : (k + 1) * LANES], 0.0
            )
            rank_here = jnp.sum(mine, 0, keepdims=True).astype(jnp.int32)
            as_hot = (r >> (bits + line_bits)) * per + rank_here
            c = r - first_cold
            as_cold = (c >> cold_bits) * per + HOT_REQ + (c & (cold_rows - 1))
            row = jnp.where(c >= 0, as_cold, as_hot)
            if k > 0:
                row = jnp.where(count[t : t + 1, :] > k - 1, row, empty)
            out[k * stride + t : k * stride + t + 1, :] = row
    for k in range(fan + 1):
        for t in range(targets, stride):
            out[k * stride + t : k * stride + t + 1, :] = empty


def plan_kernel(half, hop1, count, first, second, sizes):
    targets, seeds = count.shape

    def one_seed(s, carry):
        a, b = carry
        n = hop1[s]
        for t in range(targets):
            live = t <= n
            more = live & (count[t, s] > half - 1)
            first[a] = t * seeds + s
            second[b] = t * seeds + s
            a += live.astype(jnp.int32)
            b += more.astype(jnp.int32)
        return a, b

    a, b = lax.fori_loop(0, seeds, one_seed, (jnp.int32(0), jnp.int32(0)))
    for i in range(TASKS):
        first[a + i] = targets * seeds
        second[b + i] = targets * seeds
    sizes[0] = (a + TASKS - 1) // TASKS
    sizes[1] = (b + TASKS - 1) // TASKS


def tree(rows):
    while len(rows) > 1:
        rows = [a + b for a, b in zip(rows[::2], rows[1::2])] + (
            [rows[-1]] if len(rows) % 2 else []
        )
    return rows[0]


def finish_kernel(
    half, slots, first, second, sizes, rows, count_two, count_one,
    w_first, b_first, w_second, b_second, out, table, own, total,
):
    n_rows, width = rows.shape
    seeds, targets = count_two.shape
    step = own.shape[0]
    per = slots.shape[0] // step
    table[pl.ds(0, n_rows), :] = rows[...].astype(jnp.float32)
    table[pl.ds(n_rows, 8), :] = jnp.zeros((8, width), jnp.float32)

    def pick(k, code):
        return table[pl.ds(slots[code + k * step], 1), :]

    def first_part(i, carry):
        for g in range(TASKS):
            code = first[i * TASKS + g]
            own[pl.ds(code, 1), :] = pick(0, code)
            total[pl.ds(code, 1), :] = tree([pick(k, code) for k in range(1, half)])
        return carry

    def second_part(i, carry):
        codes = [second[i * TASKS + g] for g in range(TASKS)]
        held = [total[pl.ds(code, 1), :] for code in codes]
        sums = [
            h + tree([pick(k, code) for k in range(half, per)]) for h, code in zip(held, codes)
        ]
        for code, value in zip(codes, sums):
            total[pl.ds(code, 1), :] = value
        return carry

    lax.fori_loop(0, sizes[0], first_part, 0)
    lax.fori_loop(0, sizes[1], second_part, 0)

    pooled = jnp.zeros((seeds, w_first.shape[1]), jnp.float32)
    near = count_one[...]
    for t in range(targets):
        here = pl.ds(t * seeds, seeds)
        aggregate = total[here, :] / count_two[:, t : t + 1].astype(jnp.float32)
        stacked = jnp.concatenate(
            [own[here, :].astype(jnp.bfloat16), aggregate.astype(jnp.bfloat16)], -1
        )
        hidden = jnp.dot(stacked, w_first[...], preferred_element_type=jnp.float32) + b_first[...]
        hidden = jnp.maximum(hidden, 0.0).astype(jnp.bfloat16)
        if t == 0:
            seed_hidden = hidden
        else:
            pooled += jnp.where(near > t - 1, hidden.astype(jnp.float32), 0.0)
    pooled = (pooled / near.astype(jnp.float32)).astype(jnp.bfloat16)
    joined = jnp.concatenate([seed_hidden, pooled], -1)
    out[...] = jnp.dot(joined, w_second[...], preferred_element_type=jnp.float32) + b_second[...]


def on_device(
    hot_cache, cold_table, serve_index, serve_count, target_slot, hop2_slot,
    hop1_count, hop2_count, w_first, b_first, w_second, b_second,
):
    owners, cold_rows = serve_index.shape[1:]
    hot_dev, width = hot_cache.shape
    lines = hot_dev // LANES
    seeds, targets, fan = hop2_slot.shape
    half = (fan + 1) // 2
    step = (targets + 1) * seeds
    own_slot = target_slot.T
    near_slot = jnp.transpose(hop2_slot, (1, 2, 0))
    count_t = hop2_count.T

    rank = pl.pallas_call(
        rank_kernel,
        out_shape=jax.ShapeDtypeStruct((owners, lines, LANES), jnp.float32),
        in_specs=[VMEM, VMEM],
        out_specs=VMEM,
        name="rank",
    )(own_slot, near_slot)
    asked = lax.all_to_all(rank, "gx", split_axis=0, concat_axis=0, tiled=True)

    served_index = serve_index[0]
    slot_iota = lax.broadcasted_iota(jnp.int32, served_index.shape, 1)
    served = cold_table[served_index]
    served = jnp.where(
        (slot_iota < serve_count[0][:, None])[..., None], served, jnp.zeros((), cold_table.dtype)
    )
    answer = pl.pallas_call(
        functools.partial(select_kernel, 8 if owners % 8 == 0 else 1),
        out_shape=jax.ShapeDtypeStruct((owners, HOT_REQ + cold_rows, width), hot_cache.dtype),
        in_specs=[VMEM] * 3,
        out_specs=VMEM,
        name="select",
    )(asked, hot_cache, served)
    received = lax.all_to_all(answer, "gx", split_axis=0, concat_axis=0, tiled=True)

    slots = pl.pallas_call(
        functools.partial(remap_kernel, cold_rows),
        out_shape=jax.ShapeDtypeStruct(((fan + 1) * (targets + 1), seeds), jnp.int32),
        in_specs=[VMEM] * 4,
        out_specs=VMEM,
        name="remap",
    )(own_slot, near_slot, count_t, rank)
    first, second, sizes = pl.pallas_call(
        functools.partial(plan_kernel, half),
        out_shape=(
            jax.ShapeDtypeStruct((step,), jnp.int32),
            jax.ShapeDtypeStruct((step,), jnp.int32),
            jax.ShapeDtypeStruct((2,), jnp.int32),
        ),
        in_specs=[SMEM, SMEM],
        out_specs=(SMEM, SMEM, SMEM),
        name="plan",
    )(hop1_count, count_t)

    rows = owners * (HOT_REQ + cold_rows)
    return pl.pallas_call(
        functools.partial(finish_kernel, half),
        out_shape=jax.ShapeDtypeStruct((seeds, w_second.shape[1]), jnp.float32),
        in_specs=[SMEM] * 4 + [VMEM] * 7,
        out_specs=VMEM,
        scratch_shapes=[
            pltpu.VMEM((rows + 8, width), jnp.float32),
            pltpu.VMEM((step, width), jnp.float32),
            pltpu.VMEM((step, width), jnp.float32),
        ],
        name="finish",
    )(
        slots.reshape(-1), first, second, sizes, received.reshape(rows, width),
        hop2_count, hop1_count[:, None], w_first, b_first[None], w_second, b_second[None],
    )


def solution(mesh):
    return jax.shard_map(
        on_device,
        mesh=mesh,
        in_specs=(
            P("gx", None), P("gx", None), P("gx", None, None), P("gx", None), P("gx", None),
            P("gx", None, None), P("gx"), P("gx", None), P(), P(), P(), P(),
        ),
        out_specs=P("gx", None),
        check_vma=False,
    )
```

```python
import functools

import jax
import jax.numpy as jnp
from jax import lax
from jax.experimental import pallas as pl
from jax.experimental.pallas import tpu as pltpu
from jax.sharding import PartitionSpec as P


LANES = 128
HOT_REQ = 64
PEERS = 8
TASKS = 8

VMEM = pl.BlockSpec(memory_space=pltpu.VMEM)
SMEM = pl.BlockSpec(memory_space=pltpu.SMEM)
ANY = pl.BlockSpec(memory_space=pl.ANY)


def in_vmem(x):
    return pltpu.with_memory_space_constraint(x, pltpu.VMEM)


def split(size):
    bits = size.bit_length() - 1
    assert size == 1 << bits
    return bits


def one_hot(index, size):
    iota = lax.broadcasted_iota(jnp.int32, (size, index.shape[1]), 0)
    return jnp.where(iota == index, 1.0, 0.0).astype(jnp.bfloat16)


def rank_kernel(own, near, rank, ask, held):
    peers, groups = ask.shape[0], held.shape[0] // ask.shape[0]
    high = rank.shape[0]
    lines = high // held.shape[0]
    bits = split(LANES)
    counts = jnp.zeros((high, LANES), jnp.float32)
    for t in range(own.shape[0]):
        rows = [own[t : t + 1, :]] + [near[t, k : k + 1, :] for k in range(near.shape[1])]
        outer = jnp.concatenate([one_hot(r >> bits, high) for r in rows], 1)
        inner = jnp.concatenate([one_hot(r & (LANES - 1), LANES) for r in rows], 1)
        counts += lax.dot_general(
            outer, inner, (((1,), (1,)), ((), ())), preferred_element_type=jnp.float32
        )
    used = counts > 0.0
    flags = jnp.where(used, 1.0, 0.0).astype(jnp.bfloat16)
    a = lax.broadcasted_iota(jnp.int32, (LANES, LANES), 0)
    b = lax.broadcasted_iota(jnp.int32, (LANES, LANES), 1)
    before = jnp.where(a < b, 1.0, 0.0).astype(jnp.bfloat16)
    inside = jnp.dot(flags, before, preferred_element_type=jnp.float32)
    every = jnp.ones((LANES, LANES), jnp.bfloat16)
    sums = jnp.dot(flags, every, preferred_element_type=jnp.float32).astype(jnp.bfloat16)
    a = lax.broadcasted_iota(jnp.int32, (high, high), 0)
    b = lax.broadcasted_iota(jnp.int32, (high, high), 1)
    line_bits = split(lines)
    earlier = (a > b) & ((a >> line_bits) == (b >> line_bits))
    earlier = jnp.where(earlier, 1.0, 0.0).astype(jnp.bfloat16)
    offset = jnp.dot(earlier, sums, preferred_element_type=jnp.float32)
    value = jnp.where(used, inside + offset, -1.0)
    rank[...] = value
    held[...] = value.reshape(held.shape)
    here = lax.axis_index("gx") // peers
    for p in range(peers):
        ask[p] = jnp.concatenate([held[(here ^ g) * peers + p] for g in range(groups)], 0)


def pack_kernel(wanted, live, table, hot, *refs):
    (wide, raw, stage, sems), outs = refs[-4:], refs[:-4]
    n_hot, cold_rows = hot.shape[0], stage.shape[0]
    pieces = sems.shape[0]
    size = table.shape[0] // pieces
    copies = [
        pltpu.make_async_copy(
            table.at[pl.ds(i * size, size)], raw.at[pl.ds(i * size, size)], sems.at[i]
        )
        for i in range(pieces)
    ]
    for copy in copies:
        copy.start()
    for out in outs[1:]:
        out[pl.ds(0, n_hot), :] = hot[...]
    for i, copy in enumerate(copies):
        copy.wait()
        here = pl.ds(i * size, size)
        wide[here, :] = raw[here, :].astype(jnp.float32)
    peers = outs[0].shape[0] // cold_rows
    group = lax.axis_index("gx") // peers
    line = lax.broadcasted_iota(jnp.int32, stage.shape, 0)
    for g, out in enumerate(outs):
        base = out.shape[0] - peers * cold_rows

        def one_device(p, carry, g=g, out=out, base=base):
            d = (group ^ g) * peers + p
            for j in range(cold_rows):
                stage[j : j + 1, :] = wide[pl.ds(wanted[0, d, j], 1), :]
            kept = jnp.where(line < live[0, d], stage[...], 0.0).astype(out.dtype)
            out[pl.ds(pl.multiple_of(base + p * cold_rows, cold_rows), cold_rows), :] = kept
            return carry

        lax.fori_loop(0, peers, one_device, 0)


def select_kernel(asked, hot, *refs):
    packs, out = refs[:-1], refs[-1]
    peers = asked.shape[0]
    n_hot, groups = hot.shape[0], len(packs)
    lines = n_hot // LANES
    cold_rows = packs[0].shape[0] // peers
    want = lax.broadcasted_iota(jnp.int32, (HOT_REQ, LANES), 0).astype(jnp.float32)
    for g, pack in enumerate(packs):
        shard = hot[...] if g == 0 else pack[0:n_hot, :]
        first = pack.shape[0] - peers * cold_rows
        picks = []
        for p in range(peers):
            rows = [asked[p, g * lines + r : g * lines + r + 1, :] for r in range(lines)]
            picks.append(
                jnp.concatenate([jnp.where(want == row, 1.0, 0.0) for row in rows], 1).astype(
                    jnp.bfloat16
                )
            )
        picked = jnp.dot(
            jnp.concatenate(picks, 0), shard, preferred_element_type=jnp.float32
        ).astype(out.dtype)
        for p in range(peers):
            out[p, g * HOT_REQ : (g + 1) * HOT_REQ, :] = picked[p * HOT_REQ : (p + 1) * HOT_REQ]
            place = groups * HOT_REQ + g * cold_rows
            out[p, place : place + cold_rows, :] = pack[
                first + p * cold_rows : first + (p + 1) * cold_rows, :
            ]


def remap_kernel(peers, owners, cold_rows, half, own, near, count, ones, rank, out, place):
    high = rank.shape[0]
    targets, fan = near.shape[0], near.shape[1]
    stride = out.shape[0] // (fan + 1)
    bits, peer_bits = split(LANES), split(peers)
    owner_bits = split(high * LANES // owners)
    groups = owners // peers
    first_cold = high * LANES
    here = lax.axis_index("gx") // peers
    by_low = jnp.transpose(rank[...]).astype(jnp.bfloat16)
    low = lax.broadcasted_iota(jnp.int32, (LANES, LANES), 0)
    per = HOT_REQ + cold_rows
    cold_bits = split(cold_rows)
    empty = jnp.full((1, LANES), owners * per, jnp.int32)
    for t in range(targets):
        rows = [own[t : t + 1, :]] + [near[t, k : k + 1, :] for k in range(fan)]
        outer = jnp.concatenate([one_hot(r >> bits, high) for r in rows], 1)
        found = jnp.dot(by_low, outer, preferred_element_type=jnp.float32)
        for k, r in enumerate(rows):
            mine = jnp.where(
                low == (r & (LANES - 1)), found[:, k * LANES : (k + 1) * LANES], 0.0
            )
            rank_here = jnp.sum(mine, 0, keepdims=True).astype(jnp.int32)
            as_cold = r - first_cold
            is_cold = as_cold >= 0
            owner = jnp.where(is_cold, as_cold >> cold_bits, r >> owner_bits)
            group = (owner >> peer_bits) ^ here
            inside = jnp.where(
                is_cold,
                groups * HOT_REQ + group * cold_rows + (as_cold & (cold_rows - 1)),
                group * HOT_REQ + rank_here,
            )
            row = (owner & (peers - 1)) * (groups * per) + inside
            if k > 0:
                row = jnp.where(count[t : t + 1, :] > k - 1, row, empty)
            out[k * stride + t : k * stride + t + 1, :] = row
    for k in range(fan + 1):
        for t in range(targets, stride):
            out[k * stride + t : k * stride + t + 1, :] = empty
    node = lax.broadcasted_iota(jnp.int32, count.shape, 0)
    more = jnp.where((count[...] > half - 1) & (node <= ones[...]), 1.0, 0.0)
    a = lax.broadcasted_iota(jnp.int32, (LANES, LANES), 0)
    b = lax.broadcasted_iota(jnp.int32, (LANES, LANES), 1)
    before = jnp.where(a < b, 1.0, 0.0).astype(jnp.bfloat16)
    column = jnp.broadcast_to(jnp.sum(more, 0, keepdims=True), count.shape).astype(jnp.bfloat16)
    spot = jnp.dot(column, before, preferred_element_type=jnp.float32)
    spots, upper = [], jnp.zeros((1, LANES), jnp.float32)
    for t in range(targets):
        spots.append(spot[t : t + 1, :] + upper)
        upper = upper + more[t : t + 1, :]
    place[...] = jnp.concatenate(spots, 0).astype(jnp.int32)


def plan_kernel(hop1, place, first, second, sizes):
    seeds = hop1.shape[0]
    targets = place.shape[0] // seeds
    parts = [place.at[pl.ds(t * seeds, seeds)] for t in range(targets)]

    def one_seed(s, a):
        for t in range(targets):
            first[a + t] = t * seeds + s
        for t in range(targets):
            second[parts[t][s]] = t * seeds + s
        return a + hop1[s] + 1

    a = lax.fori_loop(0, seeds, one_seed, jnp.int32(0))
    last = targets * seeds - 1
    b = place[last] + 1
    for i in range(TASKS):
        first[a + i] = targets * seeds
        second[b + i] = targets * seeds
    sizes[0] = (a + TASKS - 1) // TASKS
    sizes[1] = (b + TASKS - 1) // TASKS


def tree(rows):
    while len(rows) > 1:
        rows = [a + b for a, b in zip(rows[::2], rows[1::2])] + (
            [rows[-1]] if len(rows) % 2 else []
        )
    return rows[0]


def finish_kernel(
    half, slots_in, first, second, sizes, rows, count_two, count_one,
    w_first_in, b_first, w_second_in, b_second, out,
    table, own, total, slots, w_first, w_second, sems,
):
    n_rows, width = rows.shape
    seeds, targets = count_two.shape
    step = own.shape[0]
    per = slots.shape[0] // step
    copies = [
        pltpu.make_async_copy(slots_in.at[here], slots.at[here], sems.at[i])
        for i, here in enumerate((pl.ds(0, half * step), pl.ds(half * step, (per - half) * step)))
    ]
    copies.append(pltpu.make_async_copy(w_first_in, w_first, sems.at[2]))
    copies.append(pltpu.make_async_copy(w_second_in, w_second, sems.at[3]))
    for copy in copies:
        copy.start()
    table[pl.ds(0, n_rows), :] = rows[...].astype(jnp.float32)
    table[pl.ds(n_rows, 8), :] = jnp.zeros((8, width), jnp.float32)
    copies[0].wait()

    parts = [slots.at[pl.ds(k * step, step)] for k in range(per)]

    def pick(k, code):
        return table[pl.ds(parts[k][code], 1), :]

    def first_part(i, carry):
        for g in range(TASKS):
            code = first[i * TASKS + g]
            own[pl.ds(code, 1), :] = pick(0, code)
            total[pl.ds(code, 1), :] = tree([pick(k, code) for k in range(1, half)])
        return carry

    def second_part(i, carry):
        codes = [second[i * TASKS + g] for g in range(TASKS)]
        held = [total[pl.ds(code, 1), :] for code in codes]
        sums = [
            h + tree([pick(k, code) for k in range(half, per)]) for h, code in zip(held, codes)
        ]
        for code, value in zip(codes, sums):
            total[pl.ds(code, 1), :] = value
        return carry

    lax.fori_loop(0, sizes[0], first_part, 0)
    copies[1].wait()
    lax.fori_loop(0, sizes[1], second_part, 0)
    copies[2].wait()
    copies[3].wait()

    pooled = jnp.zeros((seeds, w_first.shape[1]), jnp.float32)
    near = count_one[...]
    for t in range(targets):
        here = pl.ds(t * seeds, seeds)
        aggregate = total[here, :] / count_two[:, t : t + 1].astype(jnp.float32)
        stacked = jnp.concatenate(
            [own[here, :].astype(jnp.bfloat16), aggregate.astype(jnp.bfloat16)], -1
        )
        hidden = jnp.dot(stacked, w_first[...], preferred_element_type=jnp.float32) + b_first[...]
        hidden = jnp.maximum(hidden, 0.0).astype(jnp.bfloat16)
        if t == 0:
            seed_hidden = hidden
        else:
            pooled += jnp.where(near > t - 1, hidden.astype(jnp.float32), 0.0)
    pooled = (pooled / near.astype(jnp.float32)).astype(jnp.bfloat16)
    joined = jnp.concatenate([seed_hidden, pooled], -1)
    out[...] = jnp.dot(joined, w_second[...], preferred_element_type=jnp.float32) + b_second[...]


def forward(
    hot_cache, cold_table, serve_index, serve_count, target_slot, hop2_slot,
    hop1_count, hop2_count, w_first, b_first, w_second, b_second,
):
    owners, cold_rows = serve_index.shape[1:]
    hot_dev, width = hot_cache.shape
    lines = hot_dev // LANES
    peers = min(PEERS, owners)
    groups = owners // peers
    teams = [[g * peers + p for p in range(peers)] for g in range(groups)]
    seeds, targets, fan = hop2_slot.shape
    half = (fan + 1) // 2
    step = (targets + 1) * seeds
    own_slot = target_slot.T
    near_slot = jnp.transpose(hop2_slot, (1, 2, 0))
    count_t = hop2_count.T

    packs = list(pl.pallas_call(
        pack_kernel,
        out_shape=[
            jax.ShapeDtypeStruct(
                ((hot_dev if g > 0 else 0) + peers * cold_rows, width), hot_cache.dtype
            )
            for g in range(groups)
        ],
        in_specs=[SMEM, SMEM, ANY, VMEM],
        out_specs=[VMEM] * groups,
        scratch_shapes=[
            pltpu.VMEM(cold_table.shape, jnp.float32),
            pltpu.VMEM(cold_table.shape, cold_table.dtype),
            pltpu.VMEM((cold_rows, width), jnp.float32),
            pltpu.SemaphoreType.DMA((8,)),
        ],
        name="pack",
    )(serve_index, serve_count, cold_table, hot_cache))
    for g in range(1, groups):
        pairs = [(i, i ^ (g * peers)) for i in range(owners)]
        packs[g] = lax.ppermute(packs[g], "gx", pairs)

    rank, ask = pl.pallas_call(
        rank_kernel,
        out_shape=(
            jax.ShapeDtypeStruct((owners * lines, LANES), jnp.float32),
            jax.ShapeDtypeStruct((peers, groups * lines, LANES), jnp.float32),
        ),
        in_specs=[VMEM, VMEM],
        out_specs=(VMEM, VMEM),
        scratch_shapes=[pltpu.VMEM((owners, lines, LANES), jnp.float32)],
        name="rank",
    )(own_slot, near_slot)
    asked = lax.all_to_all(
        ask, "gx", split_axis=0, concat_axis=0, axis_index_groups=teams, tiled=True
    )

    answer = pl.pallas_call(
        select_kernel,
        out_shape=jax.ShapeDtypeStruct(
            (peers, groups * (HOT_REQ + cold_rows), width), hot_cache.dtype
        ),
        in_specs=[VMEM] * (2 + groups),
        out_specs=VMEM,
        name="select",
    )(in_vmem(asked), hot_cache, packs[0], *map(in_vmem, packs[1:]))
    received = lax.all_to_all(
        answer, "gx", split_axis=0, concat_axis=0, axis_index_groups=teams, tiled=True
    )

    slots, place = pl.pallas_call(
        functools.partial(remap_kernel, peers, owners, cold_rows, half),
        out_shape=(
            jax.ShapeDtypeStruct(((fan + 1) * (targets + 1), seeds), jnp.int32),
            jax.ShapeDtypeStruct((targets, seeds), jnp.int32),
        ),
        in_specs=[VMEM] * 5,
        out_specs=(VMEM, VMEM),
        name="remap",
    )(own_slot, near_slot, count_t, hop1_count[None], rank)
    first, second, sizes = pl.pallas_call(
        plan_kernel,
        out_shape=(
            jax.ShapeDtypeStruct((step,), jnp.int32),
            jax.ShapeDtypeStruct((step,), jnp.int32),
            jax.ShapeDtypeStruct((2,), jnp.int32),
        ),
        in_specs=[SMEM, SMEM],
        out_specs=(SMEM, SMEM, SMEM),
        name="plan",
    )(hop1_count, place.reshape(-1))

    rows = owners * (HOT_REQ + cold_rows)
    return pl.pallas_call(
        functools.partial(finish_kernel, half),
        out_shape=jax.ShapeDtypeStruct((seeds, w_second.shape[1]), jnp.float32),
        in_specs=[ANY] + [SMEM] * 3 + [VMEM] * 3 + [ANY, VMEM, ANY, VMEM],
        out_specs=VMEM,
        scratch_shapes=[
            pltpu.VMEM((rows + 8, width), jnp.float32),
            pltpu.VMEM((step, width), jnp.float32),
            pltpu.VMEM((step, width), jnp.float32),
            pltpu.SMEM(((fan + 1) * step,), jnp.int32),
            pltpu.VMEM(w_first.shape, w_first.dtype),
            pltpu.VMEM(w_second.shape, w_second.dtype),
            pltpu.SemaphoreType.DMA((4,)),
        ],
        name="finish",
    )(
        slots.reshape(-1), first, second, sizes, in_vmem(received.reshape(rows, width)),
        hop2_count, hop1_count[:, None],
        w_first, b_first[None], w_second, b_second[None],
    )


def solution(mesh):
    return jax.shard_map(
        forward,
        mesh=mesh,
        in_specs=(
            P("gx", None), P("gx", None), P("gx", None, None), P("gx", None), P("gx", None),
            P("gx", None, None), P("gx"), P("gx", None), P(), P(), P(), P(),
        ),
        out_specs=P("gx", None),
        check_vma=False,
    )
```

```python
import functools

import jax
import jax.numpy as jnp
from jax import lax
from jax.experimental import pallas as pl
from jax.experimental.pallas import tpu as pltpu
from jax.sharding import PartitionSpec as P


LANES = 128
HOT_REQ = 64
PEERS = 8
TASKS = 16

VMEM = pl.BlockSpec(memory_space=pltpu.VMEM)
SMEM = pl.BlockSpec(memory_space=pltpu.SMEM)
ANY = pl.BlockSpec(memory_space=pl.ANY)


def in_vmem(x):
    return pltpu.with_memory_space_constraint(x, pltpu.VMEM)


def split(size):
    bits = size.bit_length() - 1
    assert size == 1 << bits
    return bits


def one_hot(index, size):
    iota = lax.broadcasted_iota(jnp.int32, (size, index.shape[1]), 0)
    return jnp.where(iota == index, 1.0, 0.0).astype(jnp.bfloat16)


def rank_kernel(own, near, wanted, live, table, rank, ask, held, wide, raw, stage, sems):
    pieces = sems.shape[0]
    size = table.shape[0] // pieces
    copies = [
        pltpu.make_async_copy(
            table.at[pl.ds(i * size, size)], raw.at[pl.ds(i * size, size)], sems.at[i]
        )
        for i in range(pieces)
    ]
    for copy in copies:
        copy.start()
    peers, groups = ask.shape[0], held.shape[0] // ask.shape[0]
    high = rank.shape[0]
    lines = high // held.shape[0]
    bits = split(LANES)
    counts = jnp.zeros((high, LANES), jnp.float32)
    for t in range(own.shape[0]):
        rows = [own[t : t + 1, :]] + [near[t, k : k + 1, :] for k in range(near.shape[1])]
        outer = jnp.concatenate([one_hot(r >> bits, high) for r in rows], 1)
        inner = jnp.concatenate([one_hot(r & (LANES - 1), LANES) for r in rows], 1)
        counts += lax.dot_general(
            outer, inner, (((1,), (1,)), ((), ())), preferred_element_type=jnp.float32
        )
    used = counts > 0.0
    flags = jnp.where(used, 1.0, 0.0).astype(jnp.bfloat16)
    a = lax.broadcasted_iota(jnp.int32, (LANES, LANES), 0)
    b = lax.broadcasted_iota(jnp.int32, (LANES, LANES), 1)
    before = jnp.where(a < b, 1.0, 0.0).astype(jnp.bfloat16)
    inside = jnp.dot(flags, before, preferred_element_type=jnp.float32)
    every = jnp.ones((LANES, LANES), jnp.bfloat16)
    sums = jnp.dot(flags, every, preferred_element_type=jnp.float32).astype(jnp.bfloat16)
    a = lax.broadcasted_iota(jnp.int32, (high, high), 0)
    b = lax.broadcasted_iota(jnp.int32, (high, high), 1)
    line_bits = split(lines)
    earlier = (a > b) & ((a >> line_bits) == (b >> line_bits))
    earlier = jnp.where(earlier, 1.0, 0.0).astype(jnp.bfloat16)
    offset = jnp.dot(earlier, sums, preferred_element_type=jnp.float32)
    value = jnp.where(used, inside + offset, -1.0)
    rank[...] = value
    held[...] = value.reshape(held.shape)
    here = lax.axis_index("gx") // peers
    for p in range(peers):
        ask[p, 0 : groups * lines, :] = jnp.concatenate(
            [held[(here ^ g) * peers + p] for g in range(groups)], 0
        ).astype(ask.dtype)

    for i, copy in enumerate(copies):
        copy.wait()
        part = pl.ds(i * size, size)
        wide[part, :] = raw[part, :].astype(jnp.float32)
    cold_rows = stage.shape[0]
    line = lax.broadcasted_iota(jnp.int32, stage.shape, 0)
    for g in range(groups):
        place = pl.ds(groups * lines + g * cold_rows, cold_rows)

        def one_device(p, carry, g=g, place=place):
            d = (here ^ g) * peers + p
            for j in range(cold_rows):
                stage[j : j + 1, :] = wide[pl.ds(wanted[0, d, j], 1), :]
            ask[p, place, :] = jnp.where(line < live[0, d], stage[...], 0.0).astype(ask.dtype)
            return carry

        lax.fori_loop(0, peers, one_device, 0)


def select_kernel(asked, *refs):
    groups = (len(refs) - 1) // 2
    shards, out, colds = refs[:groups], refs[groups], refs[groups + 1 :]
    peers = asked.shape[0]
    lines = shards[0].shape[0] // LANES
    cold_rows = colds[0].shape[0] // peers
    want = lax.broadcasted_iota(jnp.int32, (HOT_REQ, LANES), 0).astype(jnp.float32)
    ranks = [asked[p, 0 : groups * lines, :].astype(jnp.float32) for p in range(peers)]
    for g, shard in enumerate(shards):
        picks = []
        for p in range(peers):
            rows = [ranks[p][g * lines + r : g * lines + r + 1, :] for r in range(lines)]
            picks.append(
                jnp.concatenate([jnp.where(want == row, 1.0, 0.0) for row in rows], 1).astype(
                    jnp.bfloat16
                )
            )
        picked = jnp.dot(
            jnp.concatenate(picks, 0), shard[...], preferred_element_type=jnp.float32
        ).astype(out.dtype)
        place = groups * lines + g * cold_rows
        for p in range(peers):
            out[p, g * HOT_REQ : (g + 1) * HOT_REQ, :] = picked[p * HOT_REQ : (p + 1) * HOT_REQ]
            colds[g][p * cold_rows : (p + 1) * cold_rows, :] = asked[
                p, place : place + cold_rows, :
            ]


def remap_kernel(peers, owners, cold_rows, half, own, near, count, ones, rank, out, place):
    high = rank.shape[0]
    targets, fan = near.shape[0], near.shape[1]
    stride = out.shape[0] // (fan + 1)
    bits, peer_bits = split(LANES), split(peers)
    owner_bits = split(high * LANES // owners)
    groups = owners // peers
    first_cold = high * LANES
    here = lax.axis_index("gx") // peers
    by_low = jnp.transpose(rank[...]).astype(jnp.bfloat16)
    low = lax.broadcasted_iota(jnp.int32, (LANES, LANES), 0)
    per = HOT_REQ + cold_rows
    cold_bits = split(cold_rows)
    empty = jnp.full((1, LANES), owners * per, jnp.int32)
    for t in range(targets):
        rows = [own[t : t + 1, :]] + [near[t, k : k + 1, :] for k in range(fan)]
        outer = jnp.concatenate([one_hot(r >> bits, high) for r in rows], 1)
        found = jnp.dot(by_low, outer, preferred_element_type=jnp.float32)
        for k, r in enumerate(rows):
            mine = jnp.where(
                low == (r & (LANES - 1)), found[:, k * LANES : (k + 1) * LANES], 0.0
            )
            rank_here = jnp.sum(mine, 0, keepdims=True).astype(jnp.int32)
            as_cold = r - first_cold
            is_cold = as_cold >= 0
            owner = jnp.where(is_cold, as_cold >> cold_bits, r >> owner_bits)
            group = (owner >> peer_bits) ^ here
            member = owner & (peers - 1)
            row = jnp.where(
                is_cold,
                owners * HOT_REQ
                + (group * peers + member) * cold_rows
                + (as_cold & (cold_rows - 1)),
                (member * groups + group) * HOT_REQ + rank_here,
            )
            if k > 0:
                row = jnp.where(count[t : t + 1, :] > k - 1, row, empty)
            out[k * stride + t : k * stride + t + 1, :] = row
    for k in range(fan + 1):
        for t in range(targets, stride):
            out[k * stride + t : k * stride + t + 1, :] = empty
    node = lax.broadcasted_iota(jnp.int32, count.shape, 0)
    more = jnp.where((count[...] > half - 1) & (node <= ones[...]), 1.0, 0.0)
    a = lax.broadcasted_iota(jnp.int32, (LANES, LANES), 0)
    b = lax.broadcasted_iota(jnp.int32, (LANES, LANES), 1)
    before = jnp.where(a < b, 1.0, 0.0).astype(jnp.bfloat16)
    column = jnp.broadcast_to(jnp.sum(more, 0, keepdims=True), count.shape).astype(jnp.bfloat16)
    spot = jnp.dot(column, before, preferred_element_type=jnp.float32)
    spots, upper = [], jnp.zeros((1, LANES), jnp.float32)
    for t in range(targets):
        spots.append(spot[t : t + 1, :] + upper)
        upper = upper + more[t : t + 1, :]
    place[...] = jnp.concatenate(spots, 0).astype(jnp.int32)


def plan_kernel(hop1, place, first, second, sizes):
    seeds = hop1.shape[0]
    targets = place.shape[0] // seeds
    parts = [place.at[pl.ds(t * seeds, seeds)] for t in range(targets)]

    def one_seed(s, a):
        for t in range(targets):
            first[a + t] = t * seeds + s
        for t in range(targets):
            second[parts[t][s]] = t * seeds + s
        return a + hop1[s] + 1

    a = lax.fori_loop(0, seeds, one_seed, jnp.int32(0))
    last = targets * seeds - 1
    b = place[last] + 1
    for i in range(TASKS):
        first[a + i] = targets * seeds
        second[b + i] = targets * seeds
    sizes[0] = (a + TASKS - 1) // TASKS
    sizes[1] = (b + TASKS - 1) // TASKS


def tree(rows):
    while len(rows) > 1:
        rows = [a + b for a, b in zip(rows[::2], rows[1::2])] + (
            [rows[-1]] if len(rows) % 2 else []
        )
    return rows[0]


def finish_kernel(
    half, slots_in, first, second, sizes, count_two, count_one,
    w_first_in, b_first, w_second_in, b_second, *refs,
):
    blocks = refs[:-8]
    out, table, own, total, slots, w_first, w_second, sems = refs[-8:]
    width = own.shape[1]
    seeds, targets = count_two.shape
    step = own.shape[0]
    per = slots.shape[0] // step
    copies = [
        pltpu.make_async_copy(slots_in.at[here], slots.at[here], sems.at[i])
        for i, here in enumerate((pl.ds(0, half * step), pl.ds(half * step, (per - half) * step)))
    ]
    copies.append(pltpu.make_async_copy(w_first_in, w_first, sems.at[2]))
    copies.append(pltpu.make_async_copy(w_second_in, w_second, sems.at[3]))
    for copy in copies:
        copy.start()
    n_rows = 0
    for block in blocks:
        table[pl.ds(n_rows, block.shape[0]), :] = block[...].astype(jnp.float32)
        n_rows += block.shape[0]
    table[pl.ds(n_rows, 8), :] = jnp.zeros((8, width), jnp.float32)
    copies[0].wait()

    parts = [slots.at[pl.ds(k * step, step)] for k in range(per)]

    def pick(k, code):
        return table[pl.ds(parts[k][code], 1), :]

    def first_part(i, carry):
        for g in range(TASKS):
            code = first[i * TASKS + g]
            own[pl.ds(code, 1), :] = pick(0, code)
            total[pl.ds(code, 1), :] = tree([pick(k, code) for k in range(1, half)])
        return carry

    def second_part(i, carry):
        codes = [second[i * TASKS + g] for g in range(TASKS)]
        held = [total[pl.ds(code, 1), :] for code in codes]
        sums = [
            h + tree([pick(k, code) for k in range(half, per)]) for h, code in zip(held, codes)
        ]
        for code, value in zip(codes, sums):
            total[pl.ds(code, 1), :] = value
        return carry

    lax.fori_loop(0, sizes[0], first_part, 0)
    copies[1].wait()
    lax.fori_loop(0, sizes[1], second_part, 0)
    copies[2].wait()
    copies[3].wait()

    pooled = jnp.zeros((seeds, w_first.shape[1]), jnp.float32)
    near = count_one[...]
    for t in range(targets):
        here = pl.ds(t * seeds, seeds)
        aggregate = total[here, :] / count_two[:, t : t + 1].astype(jnp.float32)
        stacked = jnp.concatenate(
            [own[here, :].astype(jnp.bfloat16), aggregate.astype(jnp.bfloat16)], -1
        )
        hidden = jnp.dot(stacked, w_first[...], preferred_element_type=jnp.float32) + b_first[...]
        hidden = jnp.maximum(hidden, 0.0).astype(jnp.bfloat16)
        if t == 0:
            seed_hidden = hidden
        else:
            pooled += jnp.where(near > t - 1, hidden.astype(jnp.float32), 0.0)
    pooled = (pooled / near.astype(jnp.float32)).astype(jnp.bfloat16)
    joined = jnp.concatenate([seed_hidden, pooled], -1)
    out[...] = jnp.dot(joined, w_second[...], preferred_element_type=jnp.float32) + b_second[...]


def forward(
    hot_cache, cold_table, serve_index, serve_count, target_slot, hop2_slot,
    hop1_count, hop2_count, w_first, b_first, w_second, b_second,
):
    owners, cold_rows = serve_index.shape[1:]
    hot_dev, width = hot_cache.shape
    lines = hot_dev // LANES
    peers = min(PEERS, owners)
    groups = owners // peers
    teams = [[g * peers + p for p in range(peers)] for g in range(groups)]
    seeds, targets, fan = hop2_slot.shape
    half = (fan + 1) // 2
    step = (targets + 1) * seeds
    own_slot = target_slot.T
    near_slot = jnp.transpose(hop2_slot, (1, 2, 0))
    count_t = hop2_count.T

    swaps = [[(i, i ^ (g * peers)) for i in range(owners)] for g in range(groups)]
    shards = [hot_cache]
    for g in range(1, groups):
        shards.append(lax.ppermute(hot_cache, "gx", swaps[g]))
    rank, ask = pl.pallas_call(
        rank_kernel,
        out_shape=(
            jax.ShapeDtypeStruct((owners * lines, LANES), jnp.float32),
            jax.ShapeDtypeStruct((peers, groups * (lines + cold_rows), width), jnp.bfloat16),
        ),
        in_specs=[VMEM, VMEM, SMEM, SMEM, ANY],
        out_specs=(VMEM, VMEM),
        scratch_shapes=[
            pltpu.VMEM((owners, lines, LANES), jnp.float32),
            pltpu.VMEM(cold_table.shape, jnp.float32),
            pltpu.VMEM(cold_table.shape, cold_table.dtype),
            pltpu.VMEM((cold_rows, width), jnp.float32),
            pltpu.SemaphoreType.DMA((8,)),
        ],
        name="rank",
    )(own_slot, near_slot, serve_index, serve_count, cold_table)
    asked = lax.all_to_all(
        ask, "gx", split_axis=0, concat_axis=0, axis_index_groups=teams, tiled=True
    )
    answer, *colds = pl.pallas_call(
        select_kernel,
        out_shape=[jax.ShapeDtypeStruct((peers, groups * HOT_REQ, width), hot_cache.dtype)]
        + [jax.ShapeDtypeStruct((peers * cold_rows, width), hot_cache.dtype)] * groups,
        in_specs=[VMEM] * (1 + groups),
        out_specs=[VMEM] * (1 + groups),
        name="select",
    )(in_vmem(asked), hot_cache, *map(in_vmem, shards[1:]))
    received = lax.all_to_all(
        answer, "gx", split_axis=0, concat_axis=0, axis_index_groups=teams, tiled=True
    )
    for g in range(1, groups):
        colds[g] = lax.ppermute(colds[g], "gx", swaps[g])

    slots, place = pl.pallas_call(
        functools.partial(remap_kernel, peers, owners, cold_rows, half),
        out_shape=(
            jax.ShapeDtypeStruct(((fan + 1) * (targets + 1), seeds), jnp.int32),
            jax.ShapeDtypeStruct((targets, seeds), jnp.int32),
        ),
        in_specs=[VMEM] * 5,
        out_specs=(VMEM, VMEM),
        name="remap",
    )(own_slot, near_slot, count_t, hop1_count[None], rank)
    first, second, sizes = pl.pallas_call(
        plan_kernel,
        out_shape=(
            jax.ShapeDtypeStruct((step,), jnp.int32),
            jax.ShapeDtypeStruct((step,), jnp.int32),
            jax.ShapeDtypeStruct((2,), jnp.int32),
        ),
        in_specs=[SMEM, SMEM],
        out_specs=(SMEM, SMEM, SMEM),
        name="plan",
    )(hop1_count, place.reshape(-1))

    rows = owners * (HOT_REQ + cold_rows)
    return pl.pallas_call(
        functools.partial(finish_kernel, half),
        out_shape=jax.ShapeDtypeStruct((seeds, w_second.shape[1]), jnp.float32),
        in_specs=[ANY] + [SMEM] * 3 + [VMEM] * 2 + [ANY, VMEM, ANY, VMEM] + [VMEM] * (1 + groups),
        out_specs=VMEM,
        scratch_shapes=[
            pltpu.VMEM((rows + 8, width), jnp.float32),
            pltpu.VMEM((step, width), jnp.float32),
            pltpu.VMEM((step, width), jnp.float32),
            pltpu.SMEM(((fan + 1) * step,), jnp.int32),
            pltpu.VMEM(w_first.shape, w_first.dtype),
            pltpu.VMEM(w_second.shape, w_second.dtype),
            pltpu.SemaphoreType.DMA((4,)),
        ],
        name="finish",
    )(
        in_vmem(slots.reshape(-1)), first, second, sizes, hop2_count, hop1_count[:, None],
        w_first, b_first[None], w_second, b_second[None],
        in_vmem(received.reshape(owners * HOT_REQ, width)), colds[0], *map(in_vmem, colds[1:]),
    )


def solution(mesh):
    return jax.shard_map(
        forward,
        mesh=mesh,
        in_specs=(
            P("gx", None), P("gx", None), P("gx", None, None), P("gx", None), P("gx", None),
            P("gx", None, None), P("gx"), P("gx", None), P(), P(), P(), P(),
        ),
        out_specs=P("gx", None),
        check_vma=False,
    )
```

```python
import functools

import jax
import jax.numpy as jnp
from jax import lax
from jax.experimental import pallas as pl
from jax.experimental.pallas import tpu as pltpu
from jax.sharding import PartitionSpec as P


LANES = 128
HOT_REQ = 64
PEERS = 8
TASKS = 32

VMEM = pl.BlockSpec(memory_space=pltpu.VMEM)
SMEM = pl.BlockSpec(memory_space=pltpu.SMEM)
ANY = pl.BlockSpec(memory_space=pl.ANY)


def in_vmem(x):
    return pltpu.with_memory_space_constraint(x, pltpu.VMEM)


def split(size):
    bits = size.bit_length() - 1
    assert size == 1 << bits
    return bits


def one_hot(index, size):
    iota = lax.broadcasted_iota(jnp.int16, (size, index.shape[1]), 0)
    wide = jnp.broadcast_to(index, iota.shape[:0] + (16, index.shape[1])).astype(jnp.int16)
    wide = jnp.concatenate([wide] * (size // 16), 0)
    one, zero = jnp.ones((), jnp.bfloat16), jnp.zeros((), jnp.bfloat16)
    return jnp.where(iota == wide, one, zero)


def rank_kernel(own, near, wanted, live, table, rank, ask, held, wide, raw, stage, sems):
    pieces = sems.shape[0]
    size = table.shape[0] // pieces
    copies = [
        pltpu.make_async_copy(
            table.at[pl.ds(i * size, size)], raw.at[pl.ds(i * size, size)], sems.at[i]
        )
        for i in range(pieces)
    ]
    for copy in copies:
        copy.start()
    peers, groups = ask.shape[0], held.shape[0] // ask.shape[0]
    high = rank.shape[0]
    lines = high // held.shape[0]
    bits = split(LANES)
    counts = jnp.zeros((high, LANES), jnp.float32)
    for t in range(own.shape[0]):
        rows = [own[t : t + 1, :]] + [near[t, k : k + 1, :] for k in range(near.shape[1])]
        outer = jnp.concatenate([one_hot(r >> bits, high) for r in rows], 1)
        inner = jnp.concatenate([one_hot(r & (LANES - 1), LANES) for r in rows], 1)
        counts += lax.dot_general(
            outer, inner, (((1,), (1,)), ((), ())), preferred_element_type=jnp.float32
        )
    used = counts > 0.0
    flags = jnp.where(used, 1.0, 0.0).astype(jnp.bfloat16)
    a = lax.broadcasted_iota(jnp.int32, (LANES, LANES), 0)
    b = lax.broadcasted_iota(jnp.int32, (LANES, LANES), 1)
    before = jnp.where(a < b, 1.0, 0.0).astype(jnp.bfloat16)
    inside = jnp.dot(flags, before, preferred_element_type=jnp.float32)
    every = jnp.ones((LANES, LANES), jnp.bfloat16)
    sums = jnp.dot(flags, every, preferred_element_type=jnp.float32).astype(jnp.bfloat16)
    a = lax.broadcasted_iota(jnp.int32, (high, high), 0)
    b = lax.broadcasted_iota(jnp.int32, (high, high), 1)
    line_bits = split(lines)
    earlier = (a > b) & ((a >> line_bits) == (b >> line_bits))
    earlier = jnp.where(earlier, 1.0, 0.0).astype(jnp.bfloat16)
    offset = jnp.dot(earlier, sums, preferred_element_type=jnp.float32)
    value = jnp.where(used, inside + offset, -1.0)
    rank[...] = value
    held[...] = value.reshape(held.shape)
    here = lax.axis_index("gx") // peers
    for p in range(peers):
        ask[p, 0 : groups * lines, :] = jnp.concatenate(
            [held[(here ^ g) * peers + p] for g in range(groups)], 0
        ).astype(ask.dtype)

    for i, copy in enumerate(copies):
        copy.wait()
        part = pl.ds(i * size, size)
        wide[part, :] = raw[part, :].astype(jnp.float32)
    cold_rows = stage.shape[0]
    line = lax.broadcasted_iota(jnp.int32, stage.shape, 0)
    for g in range(groups):
        place = pl.ds(groups * lines + g * cold_rows, cold_rows)

        def one_device(p, carry, g=g, place=place):
            d = (here ^ g) * peers + p
            for j in range(cold_rows):
                stage[j : j + 1, :] = wide[pl.ds(wanted[0, d, j], 1), :]
            ask[p, place, :] = jnp.where(line < live[0, d], stage[...], 0.0).astype(ask.dtype)
            return carry

        lax.fori_loop(0, peers, one_device, 0)


def select_kernel(asked, *refs):
    groups = (len(refs) - 1) // 2
    shards, out, colds = refs[:groups], refs[groups], refs[groups + 1 :]
    peers = asked.shape[0]
    lines = shards[0].shape[0] // LANES
    cold_rows = colds[0].shape[0] // peers
    want = lax.broadcasted_iota(jnp.int32, (HOT_REQ, LANES), 0).astype(jnp.float32)
    ranks = [asked[p, 0 : groups * lines, :].astype(jnp.float32) for p in range(peers)]
    for g, shard in enumerate(shards):
        picks = []
        for p in range(peers):
            rows = [ranks[p][g * lines + r : g * lines + r + 1, :] for r in range(lines)]
            picks.append(
                jnp.concatenate([jnp.where(want == row, 1.0, 0.0) for row in rows], 1).astype(
                    jnp.bfloat16
                )
            )
        picked = jnp.dot(
            jnp.concatenate(picks, 0), shard[...], preferred_element_type=jnp.float32
        ).astype(out.dtype)
        place = groups * lines + g * cold_rows
        for p in range(peers):
            out[p, g * HOT_REQ : (g + 1) * HOT_REQ, :] = picked[p * HOT_REQ : (p + 1) * HOT_REQ]
            colds[g][p * cold_rows : (p + 1) * cold_rows, :] = asked[
                p, place : place + cold_rows, :
            ]


def remap_kernel(peers, owners, cold_rows, half, own, near, count, ones, rank, out, place, sizes):
    high = rank.shape[0]
    targets, fan = near.shape[0], near.shape[1]
    stride = out.shape[0] // (fan + 1)
    bits, peer_bits = split(LANES), split(peers)
    owner_bits = split(high * LANES // owners)
    groups = owners // peers
    first_cold = high * LANES
    here = lax.axis_index("gx") // peers
    by_low = jnp.transpose(rank[...]).astype(jnp.bfloat16)
    low = lax.broadcasted_iota(jnp.int32, (LANES, LANES), 0)
    per = HOT_REQ + cold_rows
    cold_bits = split(cold_rows)
    empty = jnp.full((1, LANES), owners * per, jnp.int32)
    for t in range(targets):
        rows = [own[t : t + 1, :]] + [near[t, k : k + 1, :] for k in range(fan)]
        outer = jnp.concatenate([one_hot(r >> bits, high) for r in rows], 1)
        found = jnp.dot(by_low, outer, preferred_element_type=jnp.float32)
        for k, r in enumerate(rows):
            mine = jnp.where(
                low == (r & (LANES - 1)), found[:, k * LANES : (k + 1) * LANES], 0.0
            )
            rank_here = jnp.sum(mine, 0, keepdims=True).astype(jnp.int32)
            as_cold = r - first_cold
            is_cold = as_cold >= 0
            owner = jnp.where(is_cold, as_cold >> cold_bits, r >> owner_bits)
            group = (owner >> peer_bits) ^ here
            member = owner & (peers - 1)
            row = jnp.where(
                is_cold,
                owners * HOT_REQ
                + (group * peers + member) * cold_rows
                + (as_cold & (cold_rows - 1)),
                (member * groups + group) * HOT_REQ + rank_here,
            )
            if k > 0:
                row = jnp.where(count[t : t + 1, :] > k - 1, row, empty)
            out[k * stride + t : k * stride + t + 1, :] = row
    for k in range(fan + 1):
        for t in range(targets, stride):
            out[k * stride + t : k * stride + t + 1, :] = empty
    node = lax.broadcasted_iota(jnp.int32, count.shape, 0)
    more = jnp.where((count[...] > half - 1) & (node <= ones[...]), 1.0, 0.0)
    a = lax.broadcasted_iota(jnp.int32, (LANES, LANES), 0)
    b = lax.broadcasted_iota(jnp.int32, (LANES, LANES), 1)
    before = jnp.where(a < b, 1.0, 0.0).astype(jnp.bfloat16)
    column = jnp.broadcast_to(jnp.sum(more, 0, keepdims=True), count.shape).astype(jnp.bfloat16)
    spot = jnp.dot(column, before, preferred_element_type=jnp.float32)
    spots, upper = [], jnp.zeros((1, LANES), jnp.float32)
    for t in range(targets):
        spots.append(spot[t : t + 1, :] + upper)
        upper = upper + more[t : t + 1, :]
    place[...] = jnp.concatenate(spots, 0).astype(jnp.int32)
    both = jnp.concatenate(
        [count[...], ones[...], jnp.zeros((LANES - targets - 1, LANES), jnp.int32)], 0
    )
    sizes[...] = jnp.transpose(both.astype(jnp.float32))


def plan_kernel(hop1, place, first, second, sizes):
    seeds = hop1.shape[0]
    targets = place.shape[0] // seeds
    parts = [place.at[pl.ds(t * seeds, seeds)] for t in range(targets)]

    def one_seed(s, a):
        for t in range(targets):
            first[a + t] = t * seeds + s
        for t in range(targets):
            second[parts[t][s]] = t * seeds + s
        return a + hop1[s] + 1

    a = lax.fori_loop(0, seeds, one_seed, jnp.int32(0))
    last = targets * seeds - 1
    b = place[last] + 1
    for i in range(TASKS):
        first[a + i] = targets * seeds
        second[b + i] = targets * seeds
    sizes[0] = (a + TASKS - 1) // TASKS
    sizes[1] = (b + TASKS - 1) // TASKS


def tree(rows):
    while len(rows) > 1:
        rows = [a + b for a, b in zip(rows[::2], rows[1::2])] + (
            [rows[-1]] if len(rows) % 2 else []
        )
    return rows[0]


def finish_kernel(
    half, targets, slots_in, first, second, sizes, counts,
    w_first_in, b_first, w_second_in, b_second, *refs,
):
    blocks = refs[:-9]
    out, table, own, total, extra, slots, w_first, w_second, sems = refs[-9:]
    width = own.shape[1]
    seeds = counts.shape[0]
    step = own.shape[0]
    per = slots.shape[0] // step
    copies = [
        pltpu.make_async_copy(slots_in.at[here], slots.at[here], sems.at[i])
        for i, here in enumerate((pl.ds(0, half * step), pl.ds(half * step, (per - half) * step)))
    ]
    copies.append(pltpu.make_async_copy(w_first_in, w_first, sems.at[2]))
    copies.append(pltpu.make_async_copy(w_second_in, w_second, sems.at[3]))
    for copy in copies:
        copy.start()
    n_rows = 0
    for block in blocks:
        table[pl.ds(n_rows, block.shape[0]), :] = block[...].astype(jnp.float32)
        n_rows += block.shape[0]
    table[pl.ds(n_rows, 8), :] = jnp.zeros((8, width), jnp.float32)
    extra[...] = jnp.zeros(extra.shape, jnp.float32)
    copies[0].wait()

    parts = [slots.at[pl.ds(k * step, step)] for k in range(per)]

    def pick(k, code):
        return table[pl.ds(parts[k][code], 1), :]

    def first_part(i, carry):
        for g in range(TASKS):
            code = first[i * TASKS + g]
            own[pl.ds(code, 1), :] = pick(0, code)
            total[pl.ds(code, 1), :] = tree([pick(k, code) for k in range(1, half)])
        return carry

    def second_part(i, carry):
        for g in range(TASKS):
            code = second[i * TASKS + g]
            extra[pl.ds(code, 1), :] = tree([pick(k, code) for k in range(half, per)])
        return carry

    lax.fori_loop(0, sizes[0], first_part, 0)
    copies[1].wait()
    lax.fori_loop(0, sizes[1], second_part, 0)
    copies[2].wait()
    copies[3].wait()

    pooled = jnp.zeros((seeds, w_first.shape[1]), jnp.float32)
    near = counts[:, targets : targets + 1]
    for t in range(targets):
        here = pl.ds(t * seeds, seeds)
        aggregate = (total[here, :] + extra[here, :]) / counts[:, t : t + 1]
        stacked = jnp.concatenate(
            [own[here, :].astype(jnp.bfloat16), aggregate.astype(jnp.bfloat16)], -1
        )
        hidden = jnp.dot(stacked, w_first[...], preferred_element_type=jnp.float32) + b_first[...]
        hidden = jnp.maximum(hidden, 0.0).astype(jnp.bfloat16)
        if t == 0:
            seed_hidden = hidden
        else:
            pooled += jnp.where(near > t - 1, hidden.astype(jnp.float32), 0.0)
    pooled = (pooled / near).astype(jnp.bfloat16)
    joined = jnp.concatenate([seed_hidden, pooled], -1)
    out[...] = jnp.dot(joined, w_second[...], preferred_element_type=jnp.float32) + b_second[...]


def forward(
    hot_cache, cold_table, serve_index, serve_count, target_slot, hop2_slot,
    hop1_count, hop2_count, w_first, b_first, w_second, b_second,
):
    owners, cold_rows = serve_index.shape[1:]
    hot_dev, width = hot_cache.shape
    lines = hot_dev // LANES
    peers = min(PEERS, owners)
    groups = owners // peers
    teams = [[g * peers + p for p in range(peers)] for g in range(groups)]
    seeds, targets, fan = hop2_slot.shape
    half = (fan + 1) // 2
    step = (targets + 1) * seeds
    own_slot = target_slot.T
    near_slot = jnp.transpose(hop2_slot, (1, 2, 0))
    count_t = hop2_count.T

    swaps = [[(i, i ^ (g * peers)) for i in range(owners)] for g in range(groups)]
    shards = [hot_cache]
    for g in range(1, groups):
        shards.append(lax.ppermute(hot_cache, "gx", swaps[g]))
    rank, ask = pl.pallas_call(
        rank_kernel,
        out_shape=(
            jax.ShapeDtypeStruct((owners * lines, LANES), jnp.float32),
            jax.ShapeDtypeStruct((peers, groups * (lines + cold_rows), width), jnp.bfloat16),
        ),
        in_specs=[VMEM, VMEM, SMEM, SMEM, ANY],
        out_specs=(VMEM, VMEM),
        scratch_shapes=[
            pltpu.VMEM((owners, lines, LANES), jnp.float32),
            pltpu.VMEM(cold_table.shape, jnp.float32),
            pltpu.VMEM(cold_table.shape, cold_table.dtype),
            pltpu.VMEM((cold_rows, width), jnp.float32),
            pltpu.SemaphoreType.DMA((8,)),
        ],
        name="rank",
    )(own_slot, near_slot, serve_index, serve_count, cold_table)
    asked = lax.all_to_all(
        ask, "gx", split_axis=0, concat_axis=0, axis_index_groups=teams, tiled=True
    )
    answer, *colds = pl.pallas_call(
        select_kernel,
        out_shape=[jax.ShapeDtypeStruct((peers, groups * HOT_REQ, width), hot_cache.dtype)]
        + [jax.ShapeDtypeStruct((peers * cold_rows, width), hot_cache.dtype)] * groups,
        in_specs=[VMEM] * (1 + groups),
        out_specs=[VMEM] * (1 + groups),
        name="select",
    )(in_vmem(asked), in_vmem(hot_cache), *map(in_vmem, shards[1:]))
    received = lax.all_to_all(
        answer, "gx", split_axis=0, concat_axis=0, axis_index_groups=teams, tiled=True
    )
    for g in range(1, groups):
        colds[g] = lax.ppermute(colds[g], "gx", swaps[g])

    slots, place, counts = pl.pallas_call(
        functools.partial(remap_kernel, peers, owners, cold_rows, half),
        out_shape=(
            jax.ShapeDtypeStruct(((fan + 1) * (targets + 1), seeds), jnp.int32),
            jax.ShapeDtypeStruct((targets, seeds), jnp.int32),
            jax.ShapeDtypeStruct((seeds, LANES), jnp.float32),
        ),
        in_specs=[VMEM] * 5,
        out_specs=(VMEM, VMEM, VMEM),
        name="remap",
    )(own_slot, near_slot, count_t, hop1_count[None], rank)
    first, second, sizes = pl.pallas_call(
        plan_kernel,
        out_shape=(
            jax.ShapeDtypeStruct((step,), jnp.int32),
            jax.ShapeDtypeStruct((step,), jnp.int32),
            jax.ShapeDtypeStruct((2,), jnp.int32),
        ),
        in_specs=[SMEM, SMEM],
        out_specs=(SMEM, SMEM, SMEM),
        name="plan",
    )(hop1_count, place.reshape(-1))

    rows = owners * (HOT_REQ + cold_rows)
    return pl.pallas_call(
        functools.partial(finish_kernel, half, targets),
        out_shape=jax.ShapeDtypeStruct((seeds, w_second.shape[1]), jnp.float32),
        in_specs=[ANY] + [SMEM] * 3 + [VMEM] + [ANY, VMEM, ANY, VMEM] + [VMEM] * (1 + groups),
        out_specs=VMEM,
        scratch_shapes=[
            pltpu.VMEM((rows + 8, width), jnp.float32),
            pltpu.VMEM((step, width), jnp.float32),
            pltpu.VMEM((step, width), jnp.float32),
            pltpu.VMEM((step, width), jnp.float32),
            pltpu.SMEM(((fan + 1) * step,), jnp.int32),
            pltpu.VMEM(w_first.shape, w_first.dtype),
            pltpu.VMEM(w_second.shape, w_second.dtype),
            pltpu.SemaphoreType.DMA((4,)),
        ],
        name="finish",
    )(
        slots.reshape(-1), first, second, sizes, counts,
        w_first, b_first[None], w_second, b_second[None],
        in_vmem(received.reshape(owners * HOT_REQ, width)), colds[0], *map(in_vmem, colds[1:]),
    )


def solution(mesh):
    return jax.shard_map(
        forward,
        mesh=mesh,
        in_specs=(
            P("gx", None), P("gx", None), P("gx", None, None), P("gx", None), P("gx", None),
            P("gx", None, None), P("gx"), P("gx", None), P(), P(), P(), P(),
        ),
        out_specs=P("gx", None),
        check_vma=False,
    )
```

```python
import functools

import jax
import jax.numpy as jnp
from jax import lax
from jax.experimental import pallas as pl
from jax.experimental.pallas import tpu as pltpu
from jax.sharding import PartitionSpec as P


LANES = 128
HOT_REQ = 64
PEERS = 8
TASKS = 32

VMEM = pl.BlockSpec(memory_space=pltpu.VMEM)
SMEM = pl.BlockSpec(memory_space=pltpu.SMEM)
ANY = pl.BlockSpec(memory_space=pl.ANY)


def in_vmem(x):
    return pltpu.with_memory_space_constraint(x, pltpu.VMEM)


def split(size):
    bits = size.bit_length() - 1
    assert size == 1 << bits
    return bits


def one_hot(index, size):
    iota = lax.broadcasted_iota(jnp.int16, (size, index.shape[1]), 0)
    wide = jnp.broadcast_to(index, iota.shape[:0] + (16, index.shape[1])).astype(jnp.int16)
    wide = jnp.concatenate([wide] * (size // 16), 0)
    one, zero = jnp.ones((), jnp.bfloat16), jnp.zeros((), jnp.bfloat16)
    return jnp.where(iota == wide, one, zero)


def rank_kernel(
    own, near, wanted_in, live_in, table, rank_out, ask_out,
    rank, ask, held, wide, raw, stage, wanted, live, sems, sent,
):
    pieces = sems.shape[0]
    size = table.shape[0] // pieces
    copies = [
        pltpu.make_async_copy(
            table.at[pl.ds(i * size, size)], raw.at[pl.ds(i * size, size)], sems.at[i]
        )
        for i in range(pieces)
    ]
    lists = [
        pltpu.make_async_copy(source, target, sent.at[i])
        for i, (source, target) in enumerate(((wanted_in, wanted), (live_in, live)))
    ]
    for copy in lists + copies:
        copy.start()
    peers, groups = ask.shape[0], held.shape[0] // ask.shape[0]
    high = rank.shape[0]
    lines = high // held.shape[0]
    bits = split(LANES)
    counts = jnp.zeros((high, LANES), jnp.float32)
    for t in range(own.shape[0]):
        rows = [own[t : t + 1, :]] + [near[t, k : k + 1, :] for k in range(near.shape[1])]
        outer = jnp.concatenate([one_hot(r >> bits, high) for r in rows], 1)
        inner = jnp.concatenate([one_hot(r & (LANES - 1), LANES) for r in rows], 1)
        counts += lax.dot_general(
            outer, inner, (((1,), (1,)), ((), ())), preferred_element_type=jnp.float32
        )
    used = counts > 0.0
    flags = jnp.where(used, 1.0, 0.0).astype(jnp.bfloat16)
    a = lax.broadcasted_iota(jnp.int32, (LANES, LANES), 0)
    b = lax.broadcasted_iota(jnp.int32, (LANES, LANES), 1)
    before = jnp.where(a < b, 1.0, 0.0).astype(jnp.bfloat16)
    inside = jnp.dot(flags, before, preferred_element_type=jnp.float32)
    every = jnp.ones((LANES, LANES), jnp.bfloat16)
    sums = jnp.dot(flags, every, preferred_element_type=jnp.float32).astype(jnp.bfloat16)
    a = lax.broadcasted_iota(jnp.int32, (high, high), 0)
    b = lax.broadcasted_iota(jnp.int32, (high, high), 1)
    line_bits = split(lines)
    earlier = (a > b) & ((a >> line_bits) == (b >> line_bits))
    earlier = jnp.where(earlier, 1.0, 0.0).astype(jnp.bfloat16)
    offset = jnp.dot(earlier, sums, preferred_element_type=jnp.float32)
    value = jnp.where(used, inside + offset, -1.0)
    rank[...] = value
    ranks_sent = pltpu.make_async_copy(rank, rank_out, sent.at[ask.shape[0]])
    ranks_sent.start()
    held[...] = value.reshape(held.shape)
    here = lax.axis_index("gx") // peers
    for p in range(peers):
        ask[p, 0 : groups * lines, :] = jnp.concatenate(
            [held[(here ^ g) * peers + p] for g in range(groups)], 0
        ).astype(ask.dtype)

    for copy in lists:
        copy.wait()
    for i, copy in enumerate(copies):
        copy.wait()
        part = pl.ds(i * size, size)
        wide[part, :] = raw[part, :].astype(jnp.float32)
    cold_rows = stage.shape[0]
    line = lax.broadcasted_iota(jnp.int32, stage.shape, 0)
    columns = [wanted.at[:, :, pl.ds(j, cold_rows - j)] for j in range(cold_rows)]

    def one_device(p, carry):
        for g in range(groups):
            d = (here ^ g) * peers + p
            for j in range(cold_rows):
                stage[j : j + 1, :] = wide[pl.ds(columns[j][0, d, 0], 1), :]
            place = pl.ds(groups * lines + g * cold_rows, cold_rows)
            ask[p, place, :] = jnp.where(line < live[0, d], stage[...], 0.0).astype(ask.dtype)
        pltpu.make_async_copy(ask.at[p], ask_out.at[p], sent.at[p]).start()
        return carry

    lax.fori_loop(0, peers, one_device, 0)
    for p in range(peers):
        pltpu.make_async_copy(ask.at[p], ask_out.at[p], sent.at[p]).wait()
    ranks_sent.wait()


def select_kernel(asked, *refs):
    groups = (len(refs) - 3) // 2
    shards, out, colds = refs[:groups], refs[groups], refs[groups + 1 : -2]
    held, sent = refs[-2:]
    peers = asked.shape[0]
    lines = shards[0].shape[0] // LANES
    cold_rows = colds[0].shape[1]
    copies = []
    for g, cold in enumerate(colds):
        place = pl.ds(groups * lines + g * cold_rows, cold_rows)
        copies.append(pltpu.make_async_copy(asked.at[:, place], cold, sent.at[g]))
        copies[-1].start()
    want = lax.broadcasted_iota(jnp.int32, (HOT_REQ, LANES), 0).astype(jnp.float32)
    ranks = [asked[p, 0 : groups * lines, :].astype(jnp.float32) for p in range(peers)]
    for g, shard in enumerate(shards):
        picks = []
        for p in range(peers):
            rows = [ranks[p][g * lines + r : g * lines + r + 1, :] for r in range(lines)]
            picks.append(
                jnp.concatenate([jnp.where(want == row, 1.0, 0.0) for row in rows], 1).astype(
                    jnp.bfloat16
                )
            )
        picked = jnp.dot(
            jnp.concatenate(picks, 0), shard[...], preferred_element_type=jnp.float32
        ).astype(out.dtype)
        place = pl.ds(g * HOT_REQ, HOT_REQ)
        held[:, place, :] = picked.reshape(peers, HOT_REQ, picked.shape[1])
        copies.append(
            pltpu.make_async_copy(held.at[:, place], out.at[:, place], sent.at[groups + g])
        )
        copies[-1].start()
    for copy in copies:
        copy.wait()


def remap_kernel(peers, owners, cold_rows, half, own, near, count, ones, rank, out, place, sizes):
    high = rank.shape[0]
    targets, fan = near.shape[0], near.shape[1]
    stride = out.shape[0] // (fan + 1)
    bits, peer_bits = split(LANES), split(peers)
    owner_bits = split(high * LANES // owners)
    groups = owners // peers
    first_cold = high * LANES
    here = lax.axis_index("gx") // peers
    by_low = jnp.transpose(rank[...]).astype(jnp.bfloat16)
    low = lax.broadcasted_iota(jnp.int32, (LANES, LANES), 0)
    per = HOT_REQ + cold_rows
    cold_bits = split(cold_rows)
    empty = jnp.full((1, LANES), owners * per, jnp.int32)
    for t in range(targets):
        rows = [own[t : t + 1, :]] + [near[t, k : k + 1, :] for k in range(fan)]
        outer = jnp.concatenate([one_hot(r >> bits, high) for r in rows], 1)
        found = jnp.dot(by_low, outer, preferred_element_type=jnp.float32)
        for k, r in enumerate(rows):
            mine = jnp.where(
                low == (r & (LANES - 1)), found[:, k * LANES : (k + 1) * LANES], 0.0
            )
            rank_here = jnp.sum(mine, 0, keepdims=True).astype(jnp.int32)
            as_cold = r - first_cold
            is_cold = as_cold >= 0
            owner = jnp.where(is_cold, as_cold >> cold_bits, r >> owner_bits)
            group = (owner >> peer_bits) ^ here
            member = owner & (peers - 1)
            row = jnp.where(
                is_cold,
                owners * HOT_REQ
                + (group * peers + member) * cold_rows
                + (as_cold & (cold_rows - 1)),
                (member * groups + group) * HOT_REQ + rank_here,
            )
            if k > 0:
                row = jnp.where(count[t : t + 1, :] > k - 1, row, empty)
            out[k * stride + t : k * stride + t + 1, :] = row
    for k in range(fan + 1):
        for t in range(targets, stride):
            out[k * stride + t : k * stride + t + 1, :] = empty
    node = lax.broadcasted_iota(jnp.int32, count.shape, 0)
    more = jnp.where((count[...] > half - 1) & (node <= ones[...]), 1.0, 0.0)
    a = lax.broadcasted_iota(jnp.int32, (LANES, LANES), 0)
    b = lax.broadcasted_iota(jnp.int32, (LANES, LANES), 1)
    before = jnp.where(a < b, 1.0, 0.0).astype(jnp.bfloat16)
    column = jnp.broadcast_to(jnp.sum(more, 0, keepdims=True), count.shape).astype(jnp.bfloat16)
    spot = jnp.dot(column, before, preferred_element_type=jnp.float32)
    spots, upper = [], jnp.zeros((1, LANES), jnp.float32)
    for t in range(targets):
        spots.append(spot[t : t + 1, :] + upper)
        upper = upper + more[t : t + 1, :]
    place[...] = jnp.concatenate(spots, 0).astype(jnp.int32)
    both = jnp.concatenate(
        [count[...], ones[...], jnp.zeros((LANES - targets - 1, LANES), jnp.int32)], 0
    )
    sizes[...] = jnp.transpose(both.astype(jnp.float32))


def plan_kernel(hop1, place, first, second, sizes):
    seeds = hop1.shape[0]
    targets = place.shape[0] // seeds
    parts = [place.at[pl.ds(t * seeds, seeds)] for t in range(targets)]

    def one_seed(s, a):
        for t in range(targets):
            first[a + t] = t * seeds + s
        for t in range(targets):
            second[parts[t][s]] = t * seeds + s
        return a + hop1[s] + 1

    a = lax.fori_loop(0, seeds, one_seed, jnp.int32(0))
    last = targets * seeds - 1
    b = place[last] + 1
    for i in range(TASKS):
        first[a + i] = targets * seeds
        second[b + i] = targets * seeds
    sizes[0] = (a + TASKS - 1) // TASKS
    sizes[1] = (b + TASKS - 1) // TASKS


def tree(rows):
    while len(rows) > 1:
        rows = [a + b for a, b in zip(rows[::2], rows[1::2])] + (
            [rows[-1]] if len(rows) % 2 else []
        )
    return rows[0]


def finish_kernel(
    half, targets, slots_in, first_in, second_in, sizes_in, counts_in,
    w_first_in, b_first, w_second_in, b_second, *refs,
):
    blocks = refs[:-12]
    out, table, kept, extra, slots, w_first, w_second, first, second, sizes, counts, sems = refs[
        -12:
    ]
    step, width = extra.shape
    own, total = kept.at[pl.ds(0, step)], kept.at[pl.ds(step, step)]
    seeds = counts.shape[0]
    per = slots.shape[0] // step
    copies = [
        pltpu.make_async_copy(slots_in.at[here], slots.at[here], sems.at[i])
        for i, here in enumerate((pl.ds(0, half * step), pl.ds(half * step, (per - half) * step)))
    ]
    later = (
        (w_first_in, w_first), (w_second_in, w_second), (first_in, first), (second_in, second),
        (sizes_in, sizes), (counts_in, counts),
    )
    for i, (source, target) in enumerate(later):
        copies.append(pltpu.make_async_copy(source, target, sems.at[2 + i]))
    for i in (0, 4, 6, 5, 1, 2, 3, 7):
        copies[i].start()
    n_rows = 0
    for block in blocks:
        table[pl.ds(n_rows, block.shape[0]), :] = block[...].astype(jnp.float32)
        n_rows += block.shape[0]
    table[pl.ds(n_rows, 8), :] = jnp.zeros((8, width), jnp.float32)
    extra[...] = jnp.zeros(extra.shape, jnp.float32)
    for i in (0, 4, 6, 5):
        copies[i].wait()

    parts = [slots.at[pl.ds(k * step, step)] for k in range(per)]

    def pick(k, code):
        return table[pl.ds(parts[k][code], 1), :]

    def first_part(i, carry):
        for g in range(TASKS):
            code = first[i * TASKS + g]
            own[pl.ds(code, 1), :] = pick(0, code)
            total[pl.ds(code, 1), :] = tree([pick(k, code) for k in range(1, half)])
        return carry

    def second_part(i, carry):
        for g in range(TASKS):
            code = second[i * TASKS + g]
            extra[pl.ds(code, 1), :] = tree([pick(k, code) for k in range(half, per)])
        return carry

    lax.fori_loop(0, sizes[0], first_part, 0)
    copies[1].wait()
    lax.fori_loop(0, sizes[1], second_part, 0)
    copies[2].wait()
    copies[3].wait()
    copies[7].wait()

    pooled = jnp.zeros((seeds, w_first.shape[1]), jnp.float32)
    near = counts[:, targets : targets + 1]
    for t in range(targets):
        here = pl.ds(t * seeds, seeds)
        aggregate = (total[here, :] + extra[here, :]) / counts[:, t : t + 1]
        stacked = jnp.concatenate(
            [own[here, :].astype(jnp.bfloat16), aggregate.astype(jnp.bfloat16)], -1
        )
        hidden = jnp.dot(stacked, w_first[...], preferred_element_type=jnp.float32) + b_first[...]
        hidden = jnp.maximum(hidden, 0.0).astype(jnp.bfloat16)
        if t == 0:
            seed_hidden = hidden
        else:
            pooled += jnp.where(near > t - 1, hidden.astype(jnp.float32), 0.0)
    pooled = (pooled / near).astype(jnp.bfloat16)
    joined = jnp.concatenate([seed_hidden, pooled], -1)
    out[...] = jnp.dot(joined, w_second[...], preferred_element_type=jnp.float32) + b_second[...]


def forward(
    hot_cache, cold_table, serve_index, serve_count, target_slot, hop2_slot,
    hop1_count, hop2_count, w_first, b_first, w_second, b_second,
):
    owners, cold_rows = serve_index.shape[1:]
    hot_dev, width = hot_cache.shape
    lines = hot_dev // LANES
    peers = min(PEERS, owners)
    groups = owners // peers
    teams = [[g * peers + p for p in range(peers)] for g in range(groups)]
    seeds, targets, fan = hop2_slot.shape
    half = (fan + 1) // 2
    step = (targets + 1) * seeds
    own_slot = target_slot.T
    near_slot = jnp.transpose(hop2_slot, (1, 2, 0))
    count_t = hop2_count.T

    swaps = [[(i, i ^ (g * peers)) for i in range(owners)] for g in range(groups)]
    shards = [hot_cache]
    for g in range(1, groups):
        shards.append(lax.ppermute(hot_cache, "gx", swaps[g]))
    rank, ask = pl.pallas_call(
        rank_kernel,
        out_shape=(
            jax.ShapeDtypeStruct((owners * lines, LANES), jnp.float32),
            jax.ShapeDtypeStruct((peers, groups * (lines + cold_rows), width), jnp.bfloat16),
        ),
        in_specs=[VMEM, VMEM, ANY, ANY, ANY],
        out_specs=(ANY, ANY),
        scratch_shapes=[
            pltpu.VMEM((owners * lines, LANES), jnp.float32),
            pltpu.VMEM((peers, groups * (lines + cold_rows), width), jnp.bfloat16),
            pltpu.VMEM((owners, lines, LANES), jnp.float32),
            pltpu.VMEM(cold_table.shape, jnp.float32),
            pltpu.VMEM(cold_table.shape, cold_table.dtype),
            pltpu.VMEM((cold_rows, width), jnp.float32),
            pltpu.SMEM(serve_index.shape, jnp.int32),
            pltpu.SMEM(serve_count.shape, jnp.int32),
            pltpu.SemaphoreType.DMA((8,)),
            pltpu.SemaphoreType.DMA((peers + 1,)),
        ],
        name="rank",
    )(own_slot, near_slot, serve_index, serve_count, cold_table)
    asked = lax.all_to_all(
        ask, "gx", split_axis=0, concat_axis=0, axis_index_groups=teams, tiled=True
    )
    answer, *colds = pl.pallas_call(
        select_kernel,
        out_shape=[jax.ShapeDtypeStruct((peers, groups * HOT_REQ, width), hot_cache.dtype)]
        + [jax.ShapeDtypeStruct((peers, cold_rows, width), hot_cache.dtype)] * groups,
        in_specs=[VMEM] * (1 + groups),
        out_specs=[ANY] * (1 + groups),
        scratch_shapes=[
            pltpu.VMEM((peers, groups * HOT_REQ, width), hot_cache.dtype),
            pltpu.SemaphoreType.DMA((2 * groups,)),
        ],
        name="select",
    )(in_vmem(asked), in_vmem(hot_cache), *map(in_vmem, shards[1:]))
    received = lax.all_to_all(
        answer, "gx", split_axis=0, concat_axis=0, axis_index_groups=teams, tiled=True
    )
    for g in range(1, groups):
        colds[g] = lax.ppermute(colds[g], "gx", swaps[g])

    slots, place, counts = pl.pallas_call(
        functools.partial(remap_kernel, peers, owners, cold_rows, half),
        out_shape=(
            jax.ShapeDtypeStruct(((fan + 1) * (targets + 1), seeds), jnp.int32),
            jax.ShapeDtypeStruct((targets, seeds), jnp.int32),
            jax.ShapeDtypeStruct((seeds, LANES), jnp.float32),
        ),
        in_specs=[VMEM] * 5,
        out_specs=(VMEM, VMEM, VMEM),
        name="remap",
    )(own_slot, near_slot, count_t, hop1_count[None], rank)
    first, second, sizes = pl.pallas_call(
        plan_kernel,
        out_shape=(
            jax.ShapeDtypeStruct((step,), jnp.int32),
            jax.ShapeDtypeStruct((step,), jnp.int32),
            jax.ShapeDtypeStruct((2,), jnp.int32),
        ),
        in_specs=[SMEM, SMEM],
        out_specs=(SMEM, SMEM, SMEM),
        name="plan",
    )(hop1_count, place.reshape(-1))

    rows = owners * (HOT_REQ + cold_rows)
    return pl.pallas_call(
        functools.partial(finish_kernel, half, targets),
        out_shape=jax.ShapeDtypeStruct((seeds, w_second.shape[1]), jnp.float32),
        in_specs=[ANY] * 5 + [ANY, VMEM, ANY, VMEM] + [VMEM] * (1 + groups),
        out_specs=VMEM,
        scratch_shapes=[
            pltpu.VMEM((rows + 8, width), jnp.float32),
            pltpu.VMEM((2 * step, width), jnp.float32),
            pltpu.VMEM((step, width), jnp.float32),
            pltpu.SMEM(((fan + 1) * step,), jnp.int32),
            pltpu.VMEM(w_first.shape, w_first.dtype),
            pltpu.VMEM(w_second.shape, w_second.dtype),
            pltpu.SMEM((step,), jnp.int32),
            pltpu.SMEM((step,), jnp.int32),
            pltpu.SMEM((2,), jnp.int32),
            pltpu.VMEM((seeds, LANES), jnp.float32),
            pltpu.SemaphoreType.DMA((8,)),
        ],
        name="finish",
    )(
        slots.reshape(-1), first, second, sizes, counts,
        w_first, b_first[None], w_second, b_second[None],
        in_vmem(received.reshape(owners * HOT_REQ, width)),
        colds[0].reshape(-1, width), *(in_vmem(c.reshape(-1, width)) for c in colds[1:]),
    )


def solution(mesh):
    return jax.shard_map(
        forward,
        mesh=mesh,
        in_specs=(
            P("gx", None), P("gx", None), P("gx", None, None), P("gx", None), P("gx", None),
            P("gx", None, None), P("gx"), P("gx", None), P(), P(), P(), P(),
        ),
        out_specs=P("gx", None),
        check_vma=False,
    )
```

```python
import functools

import jax
import jax.numpy as jnp
from jax import lax
from jax.experimental import pallas as pl
from jax.experimental.pallas import tpu as pltpu
from jax.sharding import PartitionSpec as P


LANES = 128
HOT_REQ = 64
PEERS = 8
TASKS = 24

VMEM = pl.BlockSpec(memory_space=pltpu.VMEM)
SMEM = pl.BlockSpec(memory_space=pltpu.SMEM)
ANY = pl.BlockSpec(memory_space=pl.ANY)


def in_vmem(x):
    return pltpu.with_memory_space_constraint(x, pltpu.VMEM)


def split(size):
    bits = size.bit_length() - 1
    assert size == 1 << bits
    return bits


def one_hot(index, size):
    iota = lax.broadcasted_iota(jnp.int16, (size, index.shape[1]), 0)
    wide = jnp.broadcast_to(index, iota.shape[:0] + (16, index.shape[1])).astype(jnp.int16)
    wide = jnp.concatenate([wide] * (size // 16), 0)
    one, zero = jnp.ones((), jnp.bfloat16), jnp.zeros((), jnp.bfloat16)
    return jnp.where(iota == wide, one, zero)


def rank_kernel(
    own_in, near_in, wanted_in, live_in, table, rank_out, ask_out,
    rank, ask, held, wide, raw, stage, own, near, wanted, live, sems, sent,
):
    pieces = sems.shape[0]
    size = table.shape[0] // pieces
    copies = [
        pltpu.make_async_copy(
            table.at[pl.ds(i * size, size)], raw.at[pl.ds(i * size, size)], sems.at[i]
        )
        for i in range(pieces)
    ]
    lists = [
        pltpu.make_async_copy(source, target, sent.at[i])
        for i, (source, target) in enumerate(
            ((near_in, near), (own_in, own), (wanted_in, wanted), (live_in, live))
        )
    ]
    for copy in lists + copies:
        copy.start()
    lists[0].wait()
    lists[1].wait()
    peers, groups = ask.shape[0], held.shape[0] // ask.shape[0]
    high = rank.shape[0]
    lines = high // held.shape[0]
    bits = split(LANES)
    counts = jnp.zeros((high, LANES), jnp.float32)
    for t in range(own.shape[0]):
        rows = [own[t : t + 1, :]] + [near[t, k : k + 1, :] for k in range(near.shape[1])]
        outer = jnp.concatenate([one_hot(r >> bits, high) for r in rows], 1)
        inner = jnp.concatenate([one_hot(r & (LANES - 1), LANES) for r in rows], 1)
        counts += lax.dot_general(
            outer, inner, (((1,), (1,)), ((), ())), preferred_element_type=jnp.float32
        )
    used = counts > 0.0
    flags = jnp.where(used, 1.0, 0.0).astype(jnp.bfloat16)
    a = lax.broadcasted_iota(jnp.int32, (LANES, LANES), 0)
    b = lax.broadcasted_iota(jnp.int32, (LANES, LANES), 1)
    before = jnp.where(a < b, 1.0, 0.0).astype(jnp.bfloat16)
    inside = jnp.dot(flags, before, preferred_element_type=jnp.float32)
    every = jnp.ones((LANES, LANES), jnp.bfloat16)
    sums = jnp.dot(flags, every, preferred_element_type=jnp.float32).astype(jnp.bfloat16)
    a = lax.broadcasted_iota(jnp.int32, (high, high), 0)
    b = lax.broadcasted_iota(jnp.int32, (high, high), 1)
    line_bits = split(lines)
    earlier = (a > b) & ((a >> line_bits) == (b >> line_bits))
    earlier = jnp.where(earlier, 1.0, 0.0).astype(jnp.bfloat16)
    offset = jnp.dot(earlier, sums, preferred_element_type=jnp.float32)
    value = jnp.where(used, inside + offset, -1.0)
    rank[...] = value
    ranks_sent = pltpu.make_async_copy(rank, rank_out, sent.at[ask.shape[0]])
    ranks_sent.start()
    held[...] = value.reshape(held.shape)
    here = lax.axis_index("gx") // peers
    for p in range(peers):
        ask[p, 0 : groups * lines, :] = jnp.concatenate(
            [held[(here ^ g) * peers + p] for g in range(groups)], 0
        ).astype(ask.dtype)

    for copy in lists[2:]:
        copy.wait()
    for i, copy in enumerate(copies):
        copy.wait()
        part = pl.ds(i * size, size)
        wide[part, :] = raw[part, :].astype(jnp.float32)
    cold_rows = stage.shape[0]
    line = lax.broadcasted_iota(jnp.int32, stage.shape, 0)
    columns = [wanted.at[:, :, pl.ds(j, cold_rows - j)] for j in range(cold_rows)]

    def one_device(p, carry):
        for g in range(groups):
            d = (here ^ g) * peers + p
            for j in range(cold_rows):
                stage[j : j + 1, :] = wide[pl.ds(columns[j][0, d, 0], 1), :]
            place = pl.ds(groups * lines + g * cold_rows, cold_rows)
            ask[p, place, :] = jnp.where(line < live[0, d], stage[...], 0.0).astype(ask.dtype)
        pltpu.make_async_copy(ask.at[p], ask_out.at[p], sent.at[p]).start()
        return carry

    lax.fori_loop(0, peers, one_device, 0)
    for p in range(peers):
        pltpu.make_async_copy(ask.at[p], ask_out.at[p], sent.at[p]).wait()
    ranks_sent.wait()


def select_kernel(asked, *refs):
    groups = (len(refs) - 3) // 2
    shards, out, colds = refs[:groups], refs[groups], refs[groups + 1 : -2]
    held, sent = refs[-2:]
    peers = asked.shape[0]
    lines = shards[0].shape[0] // LANES
    cold_rows = colds[0].shape[1]
    copies = []
    for g, cold in enumerate(colds):
        place = pl.ds(groups * lines + g * cold_rows, cold_rows)
        copies.append(pltpu.make_async_copy(asked.at[:, place], cold, sent.at[g]))
        copies[-1].start()
    want = lax.broadcasted_iota(jnp.int32, (HOT_REQ, LANES), 0).astype(jnp.float32)
    ranks = [asked[p, 0 : groups * lines, :].astype(jnp.float32) for p in range(peers)]
    for g, shard in enumerate(shards):
        picks = []
        for p in range(peers):
            rows = [ranks[p][g * lines + r : g * lines + r + 1, :] for r in range(lines)]
            picks.append(
                jnp.concatenate([jnp.where(want == row, 1.0, 0.0) for row in rows], 1).astype(
                    jnp.bfloat16
                )
            )
        picked = jnp.dot(
            jnp.concatenate(picks, 0), shard[...], preferred_element_type=jnp.float32
        ).astype(out.dtype)
        place = pl.ds(g * HOT_REQ, HOT_REQ)
        held[:, place, :] = picked.reshape(peers, HOT_REQ, picked.shape[1])
        copies.append(
            pltpu.make_async_copy(held.at[:, place], out.at[:, place], sent.at[groups + g])
        )
        copies[-1].start()
    for copy in copies:
        copy.wait()


def remap_kernel(peers, owners, cold_rows, half, own, near, count, ones, rank, out, place, sizes):
    high = rank.shape[0]
    targets, fan = near.shape[0], near.shape[1]
    stride = out.shape[0] // (fan + 1)
    bits, peer_bits = split(LANES), split(peers)
    owner_bits = split(high * LANES // owners)
    groups = owners // peers
    first_cold = high * LANES
    here = lax.axis_index("gx") // peers
    by_low = jnp.transpose(rank[...]).astype(jnp.bfloat16)
    low = lax.broadcasted_iota(jnp.int32, (LANES, LANES), 0)
    per = HOT_REQ + cold_rows
    cold_bits = split(cold_rows)
    empty = jnp.full((1, LANES), owners * per, jnp.int32)
    for t in range(targets):
        rows = [own[t : t + 1, :]] + [near[t, k : k + 1, :] for k in range(fan)]
        outer = jnp.concatenate([one_hot(r >> bits, high) for r in rows], 1)
        found = jnp.dot(by_low, outer, preferred_element_type=jnp.float32)
        for k, r in enumerate(rows):
            mine = jnp.where(
                low == (r & (LANES - 1)), found[:, k * LANES : (k + 1) * LANES], 0.0
            )
            rank_here = jnp.sum(mine, 0, keepdims=True).astype(jnp.int32)
            as_cold = r - first_cold
            is_cold = as_cold >= 0
            owner = jnp.where(is_cold, as_cold >> cold_bits, r >> owner_bits)
            group = (owner >> peer_bits) ^ here
            member = owner & (peers - 1)
            row = jnp.where(
                is_cold,
                owners * HOT_REQ
                + (group * peers + member) * cold_rows
                + (as_cold & (cold_rows - 1)),
                (member * groups + group) * HOT_REQ + rank_here,
            )
            if k > 0:
                row = jnp.where(count[t : t + 1, :] > k - 1, row, empty)
            out[k * stride + t : k * stride + t + 1, :] = row
    for k in range(fan + 1):
        for t in range(targets, stride):
            out[k * stride + t : k * stride + t + 1, :] = empty
    node = lax.broadcasted_iota(jnp.int32, count.shape, 0)
    more = jnp.where((count[...] > half - 1) & (node <= ones[...]), 1.0, 0.0)
    a = lax.broadcasted_iota(jnp.int32, (LANES, LANES), 0)
    b = lax.broadcasted_iota(jnp.int32, (LANES, LANES), 1)
    before = jnp.where(a < b, 1.0, 0.0).astype(jnp.bfloat16)
    column = jnp.broadcast_to(jnp.sum(more, 0, keepdims=True), count.shape).astype(jnp.bfloat16)
    spot = jnp.dot(column, before, preferred_element_type=jnp.float32)
    spots, upper = [], jnp.zeros((1, LANES), jnp.float32)
    for t in range(targets):
        spots.append(spot[t : t + 1, :] + upper)
        upper = upper + more[t : t + 1, :]
    place[...] = jnp.concatenate(spots, 0).astype(jnp.int32)
    both = jnp.concatenate(
        [count[...], ones[...], jnp.zeros((LANES - targets - 1, LANES), jnp.int32)], 0
    )
    sizes[...] = jnp.transpose(both.astype(jnp.float32))


def plan_kernel(hop1, place, first, second, sizes):
    seeds = hop1.shape[0]
    targets = place.shape[0] // seeds
    parts = [place.at[pl.ds(t * seeds, seeds)] for t in range(targets)]

    def one_seed(s, a):
        for t in range(targets):
            first[a + t] = t * seeds + s
        for t in range(targets):
            second[parts[t][s]] = t * seeds + s
        return a + hop1[s] + 1

    a = lax.fori_loop(0, seeds, one_seed, jnp.int32(0))
    last = targets * seeds - 1
    b = place[last] + 1
    for i in range(TASKS):
        first[a + i] = targets * seeds
        second[b + i] = targets * seeds
    sizes[0] = (a + TASKS - 1) // TASKS
    sizes[1] = (b + TASKS - 1) // TASKS


def tree(rows):
    while len(rows) > 1:
        rows = [a + b for a, b in zip(rows[::2], rows[1::2])] + (
            [rows[-1]] if len(rows) % 2 else []
        )
    return rows[0]


def finish_kernel(
    half, targets, slots_in, first_in, second_in, sizes_in, counts_in,
    w_first_in, b_first_in, w_second_in, b_second_in, here_in, *refs,
):
    (
        out, table, kept, extra, slots, w_first, w_second, first, second, sizes, counts,
        b_first, b_second, here, sems,
    ) = refs[-15:]
    blocks = (refs[0], here, *refs[1:-15])
    step, width = extra.shape
    own, total = kept.at[pl.ds(0, step)], kept.at[pl.ds(step, step)]
    seeds = counts.shape[0]
    per = slots.shape[0] // step
    copies = [
        pltpu.make_async_copy(slots_in.at[part], slots.at[part], sems.at[i])
        for i, part in enumerate((pl.ds(0, half * step), pl.ds(half * step, (per - half) * step)))
    ]
    later = (
        (w_first_in, w_first), (w_second_in, w_second), (first_in, first), (second_in, second),
        (sizes_in, sizes), (counts_in, counts), (b_first_in, b_first), (b_second_in, b_second),
        (here_in, here),
    )
    for i, (source, target) in enumerate(later):
        copies.append(pltpu.make_async_copy(source, target, sems.at[2 + i]))
    for i in (0, 4, 6, 10, 5, 1, 2, 3, 7, 8, 9):
        copies[i].start()
    extra[...] = jnp.zeros(extra.shape, jnp.float32)
    n_rows = 0
    for block in blocks:
        if block is here:
            copies[10].wait()
        table[pl.ds(n_rows, block.shape[0]), :] = block[...].astype(jnp.float32)
        n_rows += block.shape[0]
    table[pl.ds(n_rows, 8), :] = jnp.zeros((8, width), jnp.float32)
    for i in (0, 4, 6, 5):
        copies[i].wait()

    parts = [slots.at[pl.ds(k * step, step)] for k in range(per)]

    def pick(k, code):
        return table[pl.ds(parts[k][code], 1), :]

    def first_part(i, carry):
        for g in range(TASKS):
            code = first[i * TASKS + g]
            own[pl.ds(code, 1), :] = pick(0, code)
            total[pl.ds(code, 1), :] = tree([pick(k, code) for k in range(1, half)])
        return carry

    def second_part(i, carry):
        for g in range(TASKS):
            code = second[i * TASKS + g]
            extra[pl.ds(code, 1), :] = tree([pick(k, code) for k in range(half, per)])
        return carry

    lax.fori_loop(0, sizes[0], first_part, 0)
    copies[1].wait()
    lax.fori_loop(0, sizes[1], second_part, 0)
    for i in (2, 3, 7, 8, 9):
        copies[i].wait()

    pooled = jnp.zeros((seeds, w_first.shape[1]), jnp.float32)
    near = counts[:, targets : targets + 1]
    for t in range(targets):
        here = pl.ds(t * seeds, seeds)
        aggregate = (total[here, :] + extra[here, :]) / counts[:, t : t + 1]
        stacked = jnp.concatenate(
            [own[here, :].astype(jnp.bfloat16), aggregate.astype(jnp.bfloat16)], -1
        )
        hidden = jnp.dot(stacked, w_first[...], preferred_element_type=jnp.float32) + b_first[...]
        hidden = jnp.maximum(hidden, 0.0).astype(jnp.bfloat16)
        if t == 0:
            seed_hidden = hidden
        else:
            pooled += jnp.where(near > t - 1, hidden.astype(jnp.float32), 0.0)
    pooled = (pooled / near).astype(jnp.bfloat16)
    joined = jnp.concatenate([seed_hidden, pooled], -1)
    out[...] = jnp.dot(joined, w_second[...], preferred_element_type=jnp.float32) + b_second[...]


def forward(
    hot_cache, cold_table, serve_index, serve_count, target_slot, hop2_slot,
    hop1_count, hop2_count, w_first, b_first, w_second, b_second,
):
    owners, cold_rows = serve_index.shape[1:]
    hot_dev, width = hot_cache.shape
    lines = hot_dev // LANES
    peers = min(PEERS, owners)
    groups = owners // peers
    teams = [[g * peers + p for p in range(peers)] for g in range(groups)]
    seeds, targets, fan = hop2_slot.shape
    half = fan // 2 + 2
    step = (targets + 1) * seeds
    own_slot = target_slot.T
    near_slot = jnp.transpose(hop2_slot, (1, 2, 0))
    count_t = hop2_count.T

    swaps = [[(i, i ^ (g * peers)) for i in range(owners)] for g in range(groups)]
    shards = [hot_cache]
    for g in range(1, groups):
        shards.append(lax.ppermute(hot_cache, "gx", swaps[g]))
    rank, ask = pl.pallas_call(
        rank_kernel,
        out_shape=(
            jax.ShapeDtypeStruct((owners * lines, LANES), jnp.float32),
            jax.ShapeDtypeStruct((peers, groups * (lines + cold_rows), width), jnp.bfloat16),
        ),
        in_specs=[ANY] * 5,
        out_specs=(ANY, ANY),
        scratch_shapes=[
            pltpu.VMEM((owners * lines, LANES), jnp.float32),
            pltpu.VMEM((peers, groups * (lines + cold_rows), width), jnp.bfloat16),
            pltpu.VMEM((owners, lines, LANES), jnp.float32),
            pltpu.VMEM(cold_table.shape, jnp.float32),
            pltpu.VMEM(cold_table.shape, cold_table.dtype),
            pltpu.VMEM((cold_rows, width), jnp.float32),
            pltpu.VMEM(own_slot.shape, jnp.int32),
            pltpu.VMEM(near_slot.shape, jnp.int32),
            pltpu.SMEM(serve_index.shape, jnp.int32),
            pltpu.SMEM(serve_count.shape, jnp.int32),
            pltpu.SemaphoreType.DMA((8,)),
            pltpu.SemaphoreType.DMA((peers + 1,)),
        ],
        name="rank",
    )(own_slot, near_slot, serve_index, serve_count, cold_table)
    asked = lax.all_to_all(
        ask, "gx", split_axis=0, concat_axis=0, axis_index_groups=teams, tiled=True
    )
    answer, *colds = pl.pallas_call(
        select_kernel,
        out_shape=[jax.ShapeDtypeStruct((peers, groups * HOT_REQ, width), hot_cache.dtype)]
        + [jax.ShapeDtypeStruct((peers, cold_rows, width), hot_cache.dtype)] * groups,
        in_specs=[VMEM] * (1 + groups),
        out_specs=[ANY] * (1 + groups),
        scratch_shapes=[
            pltpu.VMEM((peers, groups * HOT_REQ, width), hot_cache.dtype),
            pltpu.SemaphoreType.DMA((2 * groups,)),
        ],
        name="select",
    )(in_vmem(asked), in_vmem(hot_cache), *map(in_vmem, shards[1:]))
    received = lax.all_to_all(
        answer, "gx", split_axis=0, concat_axis=0, axis_index_groups=teams, tiled=True
    )
    for g in range(1, groups):
        colds[g] = lax.ppermute(colds[g], "gx", swaps[g])

    slots, place, counts = pl.pallas_call(
        functools.partial(remap_kernel, peers, owners, cold_rows, half),
        out_shape=(
            jax.ShapeDtypeStruct(((fan + 1) * (targets + 1), seeds), jnp.int32),
            jax.ShapeDtypeStruct((targets, seeds), jnp.int32),
            jax.ShapeDtypeStruct((seeds, LANES), jnp.float32),
        ),
        in_specs=[VMEM] * 5,
        out_specs=(VMEM, VMEM, VMEM),
        name="remap",
    )(own_slot, near_slot, count_t, hop1_count[None], rank)
    first, second, sizes = pl.pallas_call(
        plan_kernel,
        out_shape=(
            jax.ShapeDtypeStruct((step,), jnp.int32),
            jax.ShapeDtypeStruct((step,), jnp.int32),
            jax.ShapeDtypeStruct((2,), jnp.int32),
        ),
        in_specs=[SMEM, SMEM],
        out_specs=(SMEM, SMEM, SMEM),
        name="plan",
    )(hop1_count, place.reshape(-1))

    rows = owners * (HOT_REQ + cold_rows)
    return pl.pallas_call(
        functools.partial(finish_kernel, half, targets),
        out_shape=jax.ShapeDtypeStruct((seeds, w_second.shape[1]), jnp.float32),
        in_specs=[ANY] * 10 + [VMEM] * groups,
        out_specs=VMEM,
        scratch_shapes=[
            pltpu.VMEM((rows + 8, width), jnp.float32),
            pltpu.VMEM((2 * step, width), jnp.float32),
            pltpu.VMEM((step, width), jnp.float32),
            pltpu.SMEM(((fan + 1) * step,), jnp.int32),
            pltpu.VMEM(w_first.shape, w_first.dtype),
            pltpu.VMEM(w_second.shape, w_second.dtype),
            pltpu.SMEM((step,), jnp.int32),
            pltpu.SMEM((step,), jnp.int32),
            pltpu.SMEM((2,), jnp.int32),
            pltpu.VMEM((seeds, LANES), jnp.float32),
            pltpu.VMEM((1, b_first.shape[0]), b_first.dtype),
            pltpu.VMEM((1, b_second.shape[0]), b_second.dtype),
            pltpu.VMEM((peers * cold_rows, width), hot_cache.dtype),
            pltpu.SemaphoreType.DMA((11,)),
        ],
        name="finish",
    )(
        slots.reshape(-1), first, second, sizes, counts,
        w_first, b_first[None], w_second, b_second[None], colds[0].reshape(-1, width),
        in_vmem(received.reshape(owners * HOT_REQ, width)),
        *(in_vmem(c.reshape(-1, width)) for c in colds[1:]),
    )


def solution(mesh):
    return jax.shard_map(
        forward,
        mesh=mesh,
        in_specs=(
            P("gx", None), P("gx", None), P("gx", None, None), P("gx", None), P("gx", None),
            P("gx", None, None), P("gx"), P("gx", None), P(), P(), P(), P(),
        ),
        out_specs=P("gx", None),
        check_vma=False,
    )
```
